512 devices in a mesh: gx: 64 (over z, y), gy: 8 (over x, core).
Axes of the slice: x: 4, y: 4, z: 16, core: 2. Of those that a mesh axis runs over, the one named last changes fastest.
Arguments:
- flow_state: float32 [1, 5, 8192, 1024], P(None, None, 'gx', 'gy'), may hold values from -6 to 6
- residual: float32 [1, 5, 8192, 1024], P(None, None, 'gx', 'gy'), may hold values from -50 to 50
- speeds: float32 [1, 5, 8192, 1024], P(None, None, 'gx', 'gy'), may hold values from -2000 to 2000, as said below
- dissip: float32 [1, 8192, 1024], P(None, 'gx', 'gy'), may hold values from 0.05 to 0.5
- to_modes: float32 [5, 5, 1024], P(None, None, 'gy'), may hold values from -2.5 to 2.5
- from_modes: float32 [5, 5, 1024], P(None, None, 'gy'), may hold values from -2.5 to 2.5
Outputs:
- correction: float32 [1, 5, 8192, 1024], P(None, None, 'gx', 'gy')
The draws below stay inside these ranges and needn't reach their ends.
Inputs may be any that keep to these rules, and one draw needn't show every extreme that they name: `speeds`: magnitudes lie between 1000 and 2000; along each streamwise line (one plane, field and row) the values are positive up to some cell and negative from there on, either part possibly empty.
All inputs are finite; a program needn't handle non-finite values.
Results may differ from the reference program's by a relative error of at most 0.00011.
Values sent between devices are 32-bit elements; how exact they have to be, the bound alone decides.
A program may use at most 128 MiB of HBM per device.

```python
import math
import jax
import jax.numpy as jnp
from jax import lax

NC = 5
PL = 1
NX = 8192
NY = 1024


def draw_speeds(key, part):
    first_key, second_key, third_key = jax.random.split(key, 3)
    magnitude = jnp.exp(jax.random.uniform(first_key, (PL, NC, NX, NY), jnp.float32, math.log(1000.0), math.log(2000.0)))
    heading = jax.random.bernoulli(second_key, 0.7, (PL, NC, 1, NY))
    flip = jax.random.randint(third_key, (PL, NC, 1, NY), 0, 2 * NX)
    station = jnp.arange(NX, dtype=jnp.int32).reshape(1, 1, NX, 1)
    sign = jnp.where(heading, jnp.where(station < flip, 1.0, -1.0), -1.0)
    return (magnitude * sign).astype(jnp.float32)


def draw_residual(key, part):
    first_key = jax.random.fold_in(key, 0)
    rough = 10.0 * jax.random.normal(first_key, (PL, NC, NX, NY), jnp.float32)
    return jnp.clip(rough, -50.0, 50.0).astype(jnp.float32)


def steps_of(own_key, shape, pieces, smallest, high):
    def one(dim, blocks):
        heights = jax.random.uniform(jax.random.fold_in(jax.random.fold_in(own_key, 6), dim), (blocks,), jnp.float32, smallest / len(pieces), high / len(pieces))
        return jnp.repeat(jnp.exp(heights), shape[dim] // blocks).reshape((-1,) + (1,) * (len(shape) - dim - 1))

    factor_of = one(*pieces[0])
    for cut in pieces[1:]:
        factor_of = factor_of * one(*cut)
    return factor_of


def noise(key, dims, deviation, bound, shards=(), kind=jnp.bfloat16):
    factor_of = steps_of(key, dims, shards, -0.22, 0.18) if shards else 1.0
    values = jax.random.normal(key, dims, jnp.float32) * deviation * factor_of
    return jnp.minimum(jnp.maximum(values, -bound), bound).astype(kind)


def setup_inputs(seed: int = 0) -> dict:
    streams_of = jax.random.split(jax.random.key(seed), 7)
    flow_state = noise(streams_of[0], (PL, NC, NX, NY), 1.0, 6.0, ((2, 64), (3, 8)), jnp.float32)
    residual = draw_residual(jax.random.fold_in(streams_of[6], 71), 0)
    speeds = draw_speeds(jax.random.fold_in(streams_of[6], 71), 0)
    dissip = jnp.clip(jnp.exp(math.log(0.5) - 2.3025851 * jax.random.uniform(streams_of[3], (PL, NX, NY), jnp.float32) ** steps_of(streams_of[3], (PL, NX, NY), ((1, 64), (2, 8)), -0.2, 0.2)), 0.05, 0.5)
    to_modes = noise(streams_of[4], (NC, NC, NY), NC ** -0.5, 2.5, ((2, 8),), jnp.float32)
    from_modes = noise(streams_of[5], (NC, NC, NY), NC ** -0.5, 2.5, ((2, 8),), jnp.float32)
    return dict(flow_state=flow_state, residual=residual, speeds=speeds, dissip=dissip, to_modes=to_modes, from_modes=from_modes)


explicit_gain = 4.0
wide_share = 0.5


def fourth_diff(field, axis):
    widths = [(0, 0)] * field.ndim
    widths[axis] = (2, 2)
    padded = jnp.pad(field, widths)
    length = field.shape[axis]

    def window(k):
        return lax.slice_in_dim(padded, k, k + length, axis=axis)

    return window(0) - 4.0 * window(1) + 6.0 * window(2) - 4.0 * window(3) + window(4)


def project(matrices, field):
    summed = matrices[None, :, 0, None, :] * field[:, 0:1]
    for k in range(1, matrices.shape[1]):
        summed = summed + matrices[None, :, k, None, :] * field[:, k:k + 1]
    return summed


def band_rows(speeds, damping):
    magnitude = jnp.abs(speeds)
    near_coef = damping * magnitude
    far_coef = wide_share * near_coef
    far_low = -far_coef
    near_low = -(jnp.maximum(speeds, 0.0) + near_coef)
    centre = 1.0 + magnitude + 2.0 * near_coef + 2.0 * far_coef
    near_up = -(jnp.maximum(-speeds, 0.0) + near_coef)
    return far_low, near_low, centre, near_up, far_low


def reference(flow_state, residual, speeds, dissip, to_modes, from_modes):
    damping = dissip[:, None]
    forcing = residual - explicit_gain * damping * (fourth_diff(flow_state, 2) + fourth_diff(flow_state, 3))
    modal = project(to_modes, forcing)
    moved = (jnp.moveaxis(speeds, 2, 0), jnp.moveaxis(dissip, 1, 0), jnp.moveaxis(modal, 2, 0))
    zeros_row = jnp.zeros_like(moved[2][0])

    def forward(carried, current):
        old_one, old_two, earlier, last_one, last_two, latest = carried
        speed_row, damp_row, source_row = current
        far_low, near_low, centre, near_up, far_up = band_rows(speed_row, damp_row[:, None])
        reduced = near_low - far_low * old_one
        leading = centre - far_low * old_two
        pivot_inv = 1.0 / (leading - reduced * last_one)
        upper_one = (near_up - reduced * last_two) * pivot_inv
        upper_two = far_up * pivot_inv
        present = (source_row - far_low * earlier - reduced * latest) * pivot_inv
        return (last_one, last_two, latest, upper_one, upper_two, present), (upper_one, upper_two, present)

    start = (zeros_row, zeros_row, zeros_row, zeros_row, zeros_row, zeros_row)
    _, outputs = lax.scan(forward, start, moved)

    def backward(carried, current):
        next_one, next_two = carried
        upper_one, upper_two, present = current
        solved = present - upper_one * next_one - upper_two * next_two
        return (solved, next_one), solved

    _, solved_all = lax.scan(backward, (zeros_row, zeros_row), outputs, reverse=True)
    update = jnp.moveaxis(solved_all, 0, 2)
    return project(from_modes, update)
```

```python
import functools

import jax
import jax.numpy as jnp
from jax import lax
from jax.experimental import pallas as pl
from jax.experimental.pallas import tpu as pltpu
from jax.sharding import PartitionSpec as P

explicit_gain = 4.0
wide_share = 0.5
FIELDS = 5
ROWS = 128
LANES = 128
SUB = 8
STEPS = ROWS // SUB
LEAD = 8
SLOT = 24
BACK = 4


def mm(a, b):
    return tuple(
        tuple(a[i][0] * b[0][j] + a[i][1] * b[1][j] for j in range(2)) for i in range(2)
    )


def mv(a, v):
    return tuple(a[i][0] * v[0] + a[i][1] * v[1] for i in range(2))


def msub(a, b):
    return tuple(tuple(a[i][j] - b[i][j] for j in range(2)) for i in range(2))


def mneg(a):
    return tuple(tuple(-a[i][j] for j in range(2)) for i in range(2))


def vsub(a, b):
    return tuple(a[i] - b[i] for i in range(2))


def inverse_of_unit_less(a):
    upper = 1.0 - a[0][0]
    lower = 1.0 - a[1][1]
    scale = 1.0 / (upper * lower - a[0][1] * a[1][0])
    return ((lower * scale, a[0][1] * scale), (a[1][0] * scale, upper * scale))


def madd(a, b):
    return tuple(tuple(a[i][j] + b[i][j] for j in range(2)) for i in range(2))


def tree(fn, *items):
    return jax.tree.map(fn, *items)


def assemble(bottom, top_next):
    beta, c_mat, d_mat = bottom
    p_next, a_next, b_next = top_next
    solver = inverse_of_unit_less(mm(d_mat, a_next))
    return (
        mv(solver, vsub(beta, mv(d_mat, p_next))),
        mm(solver, c_mat),
        mneg(mm(solver, mm(d_mat, b_next))),
    )


def reduce_row(row, left, right):
    r, l_mat, r_mat = row
    solver = inverse_of_unit_less(madd(mm(l_mat, left[2]), mm(r_mat, right[1])))
    return (
        mv(solver, vsub(vsub(r, mv(l_mat, left[0])), mv(r_mat, right[0]))),
        mneg(mm(solver, mm(l_mat, left[1]))),
        mneg(mm(solver, mm(r_mat, right[2]))),
    )


def spread(row):
    return jnp.broadcast_to(row, (SUB, LANES))


def strided(ref, f, start):
    return ref[f, pl.ds(start, SUB, stride=STEPS), :]


def forcing_of(flow_ref, edge_ref, residual_ref, damp, f, j, lane):
    mid = strided(flow_ref, f, LEAD + j)
    edge = strided(edge_ref, f, j)
    stream = (
        strided(flow_ref, f, LEAD + j - 2)
        - 4.0 * strided(flow_ref, f, LEAD + j - 1)
        + 6.0 * mid
        - 4.0 * strided(flow_ref, f, LEAD + j + 1)
        + strided(flow_ref, f, LEAD + j + 2)
    )
    back_two = jnp.where(lane < 2, edge, pltpu.roll(mid, 2, 1))
    back_one = jnp.where(lane < 1, pltpu.roll(edge, LANES - 1, 1), pltpu.roll(mid, 1, 1))
    next_one = jnp.where(lane >= LANES - 1, pltpu.roll(edge, 1, 1), pltpu.roll(mid, LANES - 1, 1))
    next_two = jnp.where(lane >= LANES - 2, edge, pltpu.roll(mid, LANES - 2, 1))
    cross = back_two - 4.0 * back_one + 6.0 * mid - 4.0 * next_one + next_two
    return strided(residual_ref, f, j) - explicit_gain * damp * (stream + cross)


def eliminate(flow_ref, edge_ref, residual_ref, speeds_ref, dissip_ref, to_ref, kept_ref):
    lane = lax.broadcasted_iota(jnp.int32, (SUB, LANES), 1)
    zero = jnp.zeros((SUB, LANES), jnp.float32)
    minus = zero - 1.0
    old = [(zero, zero, zero, minus, zero) for _ in range(FIELDS)]
    last = [(zero, zero, zero, zero, minus) for _ in range(FIELDS)]
    for j in range(STEPS):
        damp = dissip_ref[pl.ds(j, SUB, stride=STEPS), :]
        forcing = [
            forcing_of(flow_ref, edge_ref, residual_ref, damp, f, j, lane) for f in range(FIELDS)
        ]
        for f in range(FIELDS):
            modal = spread(to_ref[f, 0:1, :]) * forcing[0]
            for k in range(1, FIELDS):
                modal = modal + spread(to_ref[f, k : k + 1, :]) * forcing[k]
            speed = strided(speeds_ref, f, j)
            magnitude = jnp.abs(speed)
            near = damp * magnitude
            far = wide_share * near
            near_low = -(jnp.maximum(speed, 0.0) + near)
            centre = 1.0 + magnitude + 2.0 * near + 2.0 * far
            near_up = -(jnp.maximum(-speed, 0.0) + near)
            outer = -far
            reduced = near_low - outer * old[f][0]
            leading = centre - outer * old[f][1]
            pivot_inv = 1.0 / (leading - reduced * last[f][0])
            now = (
                (near_up - reduced * last[f][1]) * pivot_inv,
                outer * pivot_inv,
                (modal - outer * old[f][2] - reduced * last[f][2]) * pivot_inv,
                -(outer * old[f][3] + reduced * last[f][3]) * pivot_inv,
                -(outer * old[f][4] + reduced * last[f][4]) * pivot_inv,
            )
            for q in range(5):
                kept_ref[f, j, q] = now[q]
            old[f], last[f] = last[f], now
    return old, last


def condense(old, last, kept_ref, rows_ref, pack_ref):
    sub = lax.broadcasted_iota(jnp.int32, (SUB, LANES), 0)
    zero = jnp.zeros((SUB, LANES), jnp.float32)
    minus = zero - 1.0
    none_vec = (zero, zero)
    none_mat = ((zero, zero), (zero, zero))
    minus_eye = ((minus, zero), (zero, minus))
    at_left = (none_vec, minus_eye, none_mat)
    at_right = (none_vec, none_mat, minus_eye)
    pack_ref[...] = jnp.zeros((LANES, LANES), jnp.float32)
    for f in range(FIELDS):
        u1a, u2a, ya, z1a, z2a = old[f]
        u1b, u2b, yb, z1b, z2b = last[f]
        beta = (ya - u1a * yb, yb)
        c_mat = ((z1a - u1a * z1b, z2a - u1a * z2b), (z1b, z2b))
        d_mat = ((u2a - u1a * u1b, -u1a * u2b), (u1b, u2b))
        nearer = (zero, zero, zero, minus, zero)
        farther = (zero, zero, zero, zero, minus)
        for j in reversed(range(STEPS - 2)):
            one = kept_ref[f, j, 0]
            two = kept_ref[f, j, 1]
            own = (kept_ref[f, j, 2], kept_ref[f, j, 3], kept_ref[f, j, 4])
            current = tuple(
                own[q] - one * nearer[q] - two * farther[q] for q in range(3)
            ) + tuple(-(one * nearer[q] + two * farther[q]) for q in range(3, 5))
            nearer, farther = current, nearer
        p_vec = (nearer[0], farther[0])
        a_mat = ((nearer[1], nearer[2]), (farther[1], farther[2]))
        b_mat = ((nearer[3], nearer[4]), (farther[3], farther[4]))
        top_next = tree(lambda a: pltpu.roll(a, SUB - 1, 0), (p_vec, a_mat, b_mat))
        row = assemble((beta, c_mat, d_mat), top_next)
        row = tree(lambda a, e: jnp.where(sub == SUB - 1, e, a), row, at_right)
        for step in (1, 2, 4):
            left = tree(lambda a, e: jnp.where(sub < step, e, pltpu.roll(a, step, 0)), row, at_left)
            right = tree(
                lambda a, e: jnp.where(sub >= SUB - 1 - step, e, pltpu.roll(a, SUB - step, 0)),
                row,
                at_right,
            )
            row = reduce_row(row, left, right)
        for q, a in enumerate(jax.tree.leaves(row)):
            rows_ref[f, q] = a
        top = (
            vsub(p_vec, mv(b_mat, row[0])),
            msub(a_mat, mm(b_mat, row[1])),
            mneg(mm(b_mat, row[2])),
        )
        before = tree(lambda a: pltpu.roll(a, 1, 0), row)
        solver = inverse_of_unit_less(mm(c_mat, before[2]))
        bottom = (
            mv(solver, vsub(beta, mv(c_mat, before[0]))),
            mneg(mm(solver, mm(c_mat, before[1]))),
            mm(solver, d_mat),
        )
        for q, a in enumerate(jax.tree.leaves(top)):
            pack_ref[f * SLOT + q : f * SLOT + q + 1, :] = a[0:1]
        for q, a in enumerate(jax.tree.leaves(bottom)):
            pack_ref[f * SLOT + 10 + q : f * SLOT + 11 + q, :] = a[SUB - 1 : SUB]


def as_relation(leaves):
    return (
        (leaves[0], leaves[1]),
        ((leaves[2], leaves[3]), (leaves[4], leaves[5])),
        ((leaves[6], leaves[7]), (leaves[8], leaves[9])),
    )


def solve_ends(pack_ref, back_ref):
    leaves = [pack_ref[pl.ds(q, FIELDS, stride=SLOT), :] for q in range(20)]
    lane = lax.broadcasted_iota(jnp.int32, (FIELDS, LANES), 1)
    top = as_relation(leaves[:10])
    bottom = as_relation(leaves[10:])
    top_next = tree(lambda a: jnp.where(lane >= LANES - 2, 0.0, pltpu.roll(a, LANES - 2, 1)), top)
    row = assemble(bottom, top_next)
    step = 2
    while step < LANES:
        left = tree(lambda a: jnp.where(lane < step, 0.0, pltpu.roll(a, step, 1)), row)
        right = tree(
            lambda a: jnp.where(lane >= LANES - step, 0.0, pltpu.roll(a, LANES - step, 1)), row
        )
        row = reduce_row(row, left, right)
        step *= 2
    own = row[0]
    behind = tree(lambda a: jnp.where(lane < 2, 0.0, pltpu.roll(a, 2, 1)), own)
    back_ref[...] = jnp.zeros((LANES, LANES), jnp.float32)
    for v, a in enumerate(behind + own):
        for f in range(FIELDS):
            back_ref[f * BACK + v : f * BACK + v + 1, :] = a[f : f + 1]


def restore(ends_ref, kept_ref, rows_ref, from_ref, out_ref):
    sub = lax.broadcasted_iota(jnp.int32, (SUB, LANES), 0)
    behind, state = [], []
    for f in range(FIELDS):
        edge = [spread(ends_ref[f * BACK + v : f * BACK + v + 1, :]) for v in range(BACK)]
        row = as_relation([rows_ref[f, q] for q in range(10)])
        cut = vsub(vsub(row[0], mv(row[1], edge[:2])), mv(row[2], edge[2:]))
        behind.append(
            tuple(jnp.where(sub == 0, edge[v], pltpu.roll(cut[v], 1, 0)) for v in range(2))
        )
        state.append(cut)
    for j in reversed(range(STEPS)):
        update = []
        for f in range(FIELDS):
            if j >= STEPS - 2:
                update.append(state[f][j - (STEPS - 2)])
                continue
            nearer, farther = state[f]
            current = (
                kept_ref[f, j, 2]
                - kept_ref[f, j, 3] * behind[f][0]
                - kept_ref[f, j, 4] * behind[f][1]
                - kept_ref[f, j, 1] * farther
                - kept_ref[f, j, 0] * nearer
            )
            state[f] = (current, nearer)
            update.append(current)
        for k in range(FIELDS):
            total = spread(from_ref[k, 0:1, :]) * update[0]
            for m in range(1, FIELDS):
                total = total + spread(from_ref[k, m : m + 1, :]) * update[m]
            out_ref[k, pl.ds(j, SUB, stride=STEPS), :] = total


def local_kernel(flow, edge, residual, speeds, dissip, to_modes, sent, kept, rows, pack):
    old, last = eliminate(flow, edge, residual, speeds, dissip, to_modes, kept)
    condense(old, last, kept, rows, pack)
    sent[...] = pack[...].T


def ends_kernel(got, sent, pack, back):
    pack[...] = got[...].T
    solve_ends(pack, back)
    sent[...] = back[...].T


def final_kernel(got, kept, rows, from_modes, out, ends):
    ends[...] = got[...].T
    restore(ends, kept, rows, from_modes, out)


VM = pl.BlockSpec(memory_space=pltpu.VMEM)
f32 = jnp.float32
SQUARE = jax.ShapeDtypeStruct((LANES, LANES), f32)


def call(kernel, count, outs, scratch, interpret=False):
    return pl.pallas_call(
        kernel,
        out_shape=outs,
        in_specs=[VM] * count,
        out_specs=jax.tree.map(lambda _: VM, outs),
        scratch_shapes=scratch,
        interpret=interpret,
        compiler_params=pltpu.CompilerParams(vmem_limit_bytes=48 << 20),
    )


def stage_one(*args, interpret=False):
    outs = (
        SQUARE,
        jax.ShapeDtypeStruct((FIELDS, STEPS, 5, SUB, LANES), f32),
        jax.ShapeDtypeStruct((FIELDS, 10, SUB, LANES), f32),
    )
    return call(local_kernel, 6, outs, [pltpu.VMEM((LANES, LANES), f32)], interpret)(*args)


def stage_two(got, interpret=False):
    return call(ends_kernel, 1, SQUARE, [pltpu.VMEM((LANES, LANES), f32)] * 2, interpret)(got)


def stage_three(*args, interpret=False):
    outs = jax.ShapeDtypeStruct((FIELDS, ROWS, LANES), f32)
    return call(final_kernel, 4, outs, [pltpu.VMEM((LANES, LANES), f32)], interpret)(*args)


def shifted(a, axis, up):
    count = lax.axis_size(axis)
    pairs = [(i, i + 1) if up else (i + 1, i) for i in range(count - 1)]
    return lax.ppermute(a, axis, pairs)


def exchange(a, blocks):
    split = a.reshape(blocks, LANES // blocks, LANES)
    return lax.all_to_all(split, "gx", 0, 0).reshape(LANES, LANES)


def local(flow_state, residual, speeds, dissip, to_modes, from_modes):
    blocks = lax.axis_size("gx")
    flow = flow_state[0]
    above = shifted(flow[:, ROWS - LEAD :], "gx", True)
    below = shifted(flow[:, :LEAD], "gx", False)
    flipped = jnp.swapaxes(flow, 1, 2)
    before = shifted(flipped[:, LANES - 2 :], "gy", True)
    after = shifted(flipped[:, :2], "gy", False)
    padded = jnp.concatenate([above, flow, below], axis=1)
    edge = jnp.concatenate(
        [
            jnp.swapaxes(before, 1, 2),
            jnp.zeros((FIELDS, ROWS, LANES - 4), f32),
            jnp.swapaxes(after, 1, 2),
        ],
        axis=2,
    )
    sent, kept, rows = stage_one(padded, edge, residual[0], speeds[0], dissip[0], to_modes)
    back = stage_two(exchange(sent, blocks))
    return stage_three(exchange(back, blocks), kept, rows, from_modes)[None]


def solution(mesh):
    placed = (
        P(None, None, "gx", "gy"),
        P(None, None, "gx", "gy"),
        P(None, None, "gx", "gy"),
        P(None, "gx", "gy"),
        P(None, None, "gy"),
        P(None, None, "gy"),
    )
    return jax.shard_map(
        local, mesh=mesh, in_specs=placed, out_specs=P(None, None, "gx", "gy"), check_vma=False
    )
```

```python
import jax
import jax.numpy as jnp
from jax import lax
from jax.experimental import pallas as pl
from jax.experimental.pallas import tpu as pltpu
from jax.sharding import PartitionSpec as P

explicit_gain = 4.0
wide_share = 0.5
FIELDS = 5
ROWS = 128
LANES = 128
SUB = 8
STEPS = ROWS // SUB
LEAD = 8
SLOT = 24
BACK = 4


def mm(a, b):
    return tuple(
        tuple(a[i][0] * b[0][j] + a[i][1] * b[1][j] for j in range(2)) for i in range(2)
    )


def mv(a, v):
    return tuple(a[i][0] * v[0] + a[i][1] * v[1] for i in range(2))


def msub(a, b):
    return tuple(tuple(a[i][j] - b[i][j] for j in range(2)) for i in range(2))


def mneg(a):
    return tuple(tuple(-a[i][j] for j in range(2)) for i in range(2))


def vsub(a, b):
    return tuple(a[i] - b[i] for i in range(2))


def inverse_of_unit_less(a):
    upper = 1.0 - a[0][0]
    lower = 1.0 - a[1][1]
    scale = 1.0 / (upper * lower - a[0][1] * a[1][0])
    return ((lower * scale, a[0][1] * scale), (a[1][0] * scale, upper * scale))


def madd(a, b):
    return tuple(tuple(a[i][j] + b[i][j] for j in range(2)) for i in range(2))


def tree(fn, *items):
    return jax.tree.map(fn, *items)


def assemble(bottom, top_next):
    beta, c_mat, d_mat = bottom
    p_next, a_next, b_next = top_next
    solver = inverse_of_unit_less(mm(d_mat, a_next))
    return (
        mv(solver, vsub(beta, mv(d_mat, p_next))),
        mm(solver, c_mat),
        mneg(mm(solver, mm(d_mat, b_next))),
    )


def reduce_row(row, left, right):
    r, l_mat, r_mat = row
    solver = inverse_of_unit_less(madd(mm(l_mat, left[2]), mm(r_mat, right[1])))
    return (
        mv(solver, vsub(vsub(r, mv(l_mat, left[0])), mv(r_mat, right[0]))),
        mneg(mm(solver, mm(l_mat, left[1]))),
        mneg(mm(solver, mm(r_mat, right[2]))),
    )


def spread(row):
    return jnp.broadcast_to(row, (SUB, LANES))


def strided(ref, f, start):
    return ref[f, pl.ds(start, SUB, stride=STEPS), :]


def forcing_of(flow_ref, edge, residual_ref, damp, f, j, lane):
    mid = strided(flow_ref, f, LEAD + j)
    stream = (
        strided(flow_ref, f, LEAD + j - 2)
        - 4.0 * strided(flow_ref, f, LEAD + j - 1)
        + 6.0 * mid
        - 4.0 * strided(flow_ref, f, LEAD + j + 1)
        + strided(flow_ref, f, LEAD + j + 2)
    )
    back_two = jnp.where(lane < 2, edge, pltpu.roll(mid, 2, 1))
    back_one = jnp.where(lane < 1, pltpu.roll(edge, LANES - 1, 1), pltpu.roll(mid, 1, 1))
    next_one = jnp.where(lane >= LANES - 1, pltpu.roll(edge, 1, 1), pltpu.roll(mid, LANES - 1, 1))
    next_two = jnp.where(lane >= LANES - 2, edge, pltpu.roll(mid, LANES - 2, 1))
    cross = back_two - 4.0 * back_one + 6.0 * mid - 4.0 * next_one + next_two
    return strided(residual_ref, f, j) - explicit_gain * damp * (stream + cross)


def factor(speeds_ref, dissip_ref, kept_ref, scale_ref):
    zero = jnp.zeros((SUB, LANES), jnp.float32)
    minus = zero - 1.0
    old = [(zero, zero, minus, zero) for _ in range(FIELDS)]
    last = [(zero, zero, zero, minus) for _ in range(FIELDS)]
    for j in range(STEPS):
        damp = dissip_ref[pl.ds(j, SUB, stride=STEPS), :]
        for f in range(FIELDS):
            speed = strided(speeds_ref, f, j)
            magnitude = jnp.abs(speed)
            near = damp * magnitude
            far = wide_share * near
            near_low = -(jnp.maximum(speed, 0.0) + near)
            centre = 1.0 + magnitude + 2.0 * near + 2.0 * far
            near_up = -(jnp.maximum(-speed, 0.0) + near)
            outer = -far
            reduced = near_low - outer * old[f][0]
            leading = centre - outer * old[f][1]
            pivot_inv = 1.0 / (leading - reduced * last[f][0])
            upper_two = outer * pivot_inv
            low = reduced * pivot_inv
            now = (
                (near_up - reduced * last[f][1]) * pivot_inv,
                upper_two,
                -(upper_two * old[f][2] + low * last[f][2]),
                -(upper_two * old[f][3] + low * last[f][3]),
            )
            for q in range(4):
                kept_ref[f, j, q] = now[q]
            scale_ref[f, j, 0] = pivot_inv
            scale_ref[f, j, 1] = low
            old[f], last[f] = last[f], now


def sweep(flow_ref, edge_ref, residual_ref, dissip_ref, to_ref, kept_ref, scale_ref):
    lane = lax.broadcasted_iota(jnp.int32, (SUB, LANES), 1)
    zero = jnp.zeros((SUB, LANES), jnp.float32)
    old = [zero] * FIELDS
    last = [zero] * FIELDS
    for j in range(STEPS):
        damp = dissip_ref[pl.ds(j, SUB, stride=STEPS), :]
        edges = edge_ref[pl.ds(j, SUB, stride=STEPS), :]
        forcing = [
            forcing_of(
                flow_ref,
                pltpu.roll(edges, LANES - 2 - SUB * f, 1),
                residual_ref,
                damp,
                f,
                j,
                lane,
            )
            for f in range(FIELDS)
        ]
        for f in range(FIELDS):
            modal = spread(to_ref[f, 0:1, :]) * forcing[0]
            for k in range(1, FIELDS):
                modal = modal + spread(to_ref[f, k : k + 1, :]) * forcing[k]
            now = (
                modal * scale_ref[f, j, 0]
                - kept_ref[f, j, 1] * old[f]
                - scale_ref[f, j, 1] * last[f]
            )
            kept_ref[f, j, 4] = now
            old[f], last[f] = last[f], now


def condense(kept_ref, rows_ref, pack_ref):
    sub = lax.broadcasted_iota(jnp.int32, (SUB, LANES), 0)
    zero = jnp.zeros((SUB, LANES), jnp.float32)
    minus = zero - 1.0
    none_vec = (zero, zero)
    none_mat = ((zero, zero), (zero, zero))
    minus_eye = ((minus, zero), (zero, minus))
    at_left = (none_vec, minus_eye, none_mat)
    at_right = (none_vec, none_mat, minus_eye)
    pack_ref[...] = jnp.zeros((LANES, LANES), jnp.float32)
    for f in range(FIELDS):
        u1a, u2a, z1a, z2a, ya = (kept_ref[f, STEPS - 2, q] for q in range(5))
        u1b, u2b, z1b, z2b, yb = (kept_ref[f, STEPS - 1, q] for q in range(5))
        beta = (ya - u1a * yb, yb)
        c_mat = ((z1a - u1a * z1b, z2a - u1a * z2b), (z1b, z2b))
        d_mat = ((u2a - u1a * u1b, -u1a * u2b), (u1b, u2b))
        nearer = (zero, zero, zero, minus, zero)
        farther = (zero, zero, zero, zero, minus)
        for j in reversed(range(STEPS - 2)):
            one = kept_ref[f, j, 0]
            two = kept_ref[f, j, 1]
            own = (kept_ref[f, j, 4], kept_ref[f, j, 2], kept_ref[f, j, 3])
            current = tuple(
                own[q] - one * nearer[q] - two * farther[q] for q in range(3)
            ) + tuple(-(one * nearer[q] + two * farther[q]) for q in range(3, 5))
            nearer, farther = current, nearer
        p_vec = (nearer[0], farther[0])
        a_mat = ((nearer[1], nearer[2]), (farther[1], farther[2]))
        b_mat = ((nearer[3], nearer[4]), (farther[3], farther[4]))
        top_next = tree(lambda a: pltpu.roll(a, SUB - 1, 0), (p_vec, a_mat, b_mat))
        row = assemble((beta, c_mat, d_mat), top_next)
        row = tree(lambda a, e: jnp.where(sub == SUB - 1, e, a), row, at_right)
        for step in (1, 2, 4):
            left = tree(lambda a, e: jnp.where(sub < step, e, pltpu.roll(a, step, 0)), row, at_left)
            right = tree(
                lambda a, e: jnp.where(sub >= SUB - 1 - step, e, pltpu.roll(a, SUB - step, 0)),
                row,
                at_right,
            )
            row = reduce_row(row, left, right)
        for q, a in enumerate(jax.tree.leaves(row)):
            rows_ref[f, q] = a
        top = (
            vsub(p_vec, mv(b_mat, row[0])),
            msub(a_mat, mm(b_mat, row[1])),
            mneg(mm(b_mat, row[2])),
        )
        before = tree(lambda a: pltpu.roll(a, 1, 0), row)
        solver = inverse_of_unit_less(mm(c_mat, before[2]))
        bottom = (
            mv(solver, vsub(beta, mv(c_mat, before[0]))),
            mneg(mm(solver, mm(c_mat, before[1]))),
            mm(solver, d_mat),
        )
        for q, a in enumerate(jax.tree.leaves(top)):
            pack_ref[f * SLOT + q : f * SLOT + q + 1, :] = a[0:1]
        for q, a in enumerate(jax.tree.leaves(bottom)):
            pack_ref[f * SLOT + 10 + q : f * SLOT + 11 + q, :] = a[SUB - 1 : SUB]


def as_relation(leaves):
    return (
        (leaves[0], leaves[1]),
        ((leaves[2], leaves[3]), (leaves[4], leaves[5])),
        ((leaves[6], leaves[7]), (leaves[8], leaves[9])),
    )


def solve_ends(pack_ref, back_ref):
    leaves = [pack_ref[pl.ds(q, FIELDS, stride=SLOT), :] for q in range(20)]
    lane = lax.broadcasted_iota(jnp.int32, (FIELDS, LANES), 1)
    top = as_relation(leaves[:10])
    bottom = as_relation(leaves[10:])
    top_next = tree(lambda a: jnp.where(lane >= LANES - 2, 0.0, pltpu.roll(a, LANES - 2, 1)), top)
    row = assemble(bottom, top_next)
    step = 2
    while step < LANES:
        left = tree(lambda a: jnp.where(lane < step, 0.0, pltpu.roll(a, step, 1)), row)
        right = tree(
            lambda a: jnp.where(lane >= LANES - step, 0.0, pltpu.roll(a, LANES - step, 1)), row
        )
        row = reduce_row(row, left, right)
        step *= 2
    own = row[0]
    behind = tree(lambda a: jnp.where(lane < 2, 0.0, pltpu.roll(a, 2, 1)), own)
    back_ref[...] = jnp.zeros((LANES, LANES), jnp.float32)
    for v, a in enumerate(behind + own):
        for f in range(FIELDS):
            back_ref[f * BACK + v : f * BACK + v + 1, :] = a[f : f + 1]


def restore(ends_ref, kept_ref, rows_ref, from_ref, out_ref):
    sub = lax.broadcasted_iota(jnp.int32, (SUB, LANES), 0)
    behind, state = [], []
    for f in range(FIELDS):
        edge = [spread(ends_ref[f * BACK + v : f * BACK + v + 1, :]) for v in range(BACK)]
        row = as_relation([rows_ref[f, q] for q in range(10)])
        cut = vsub(vsub(row[0], mv(row[1], edge[:2])), mv(row[2], edge[2:]))
        behind.append(
            tuple(jnp.where(sub == 0, edge[v], pltpu.roll(cut[v], 1, 0)) for v in range(2))
        )
        state.append(cut)
    for j in reversed(range(STEPS)):
        update = []
        for f in range(FIELDS):
            if j >= STEPS - 2:
                update.append(state[f][j - (STEPS - 2)])
                continue
            nearer, farther = state[f]
            current = (
                kept_ref[f, j, 4]
                - kept_ref[f, j, 2] * behind[f][0]
                - kept_ref[f, j, 3] * behind[f][1]
                - kept_ref[f, j, 1] * farther
                - kept_ref[f, j, 0] * nearer
            )
            state[f] = (current, nearer)
            update.append(current)
        for k in range(FIELDS):
            total = spread(from_ref[k, 0:1, :]) * update[0]
            for m in range(1, FIELDS):
                total = total + spread(from_ref[k, m : m + 1, :]) * update[m]
            out_ref[k, pl.ds(j, SUB, stride=STEPS), :] = total


ALONG_Y = 4
ALONG_Z = 16
GX = ALONG_Y * ALONG_Z
GY = 8
MESH = pl.DeviceIdType.MESH
EDGES = FIELDS * SUB


def pack_edges(flow_ref, square_ref, sent_ref):
    lane = lax.broadcasted_iota(jnp.int32, (ROWS, LANES), 1)
    total = jnp.zeros((ROWS, LANES), jnp.float32)
    for f in range(FIELDS):
        mid = flow_ref[f, LEAD : LEAD + ROWS, :]
        at = lane - SUB * f
        total = jnp.where((at >= 0) & (at < 2), pltpu.roll(mid, SUB * f, 1) if f else mid, total)
        total = jnp.where((at >= 2) & (at < 4), pltpu.roll(mid, SUB * f + 4, 1), total)
    square_ref[...] = total.T
    sent_ref[...] = square_ref[0:EDGES, :]


def unpack_edges(got_ref, square_ref):
    row = lax.broadcasted_iota(jnp.int32, (EDGES, LANES), 0)
    square_ref[...] = jnp.zeros((LANES, LANES), jnp.float32)
    square_ref[0:EDGES, :] = jnp.where(lax.rem(row, SUB) < 2, got_ref[1], got_ref[0])
    square_ref[...] = square_ref[...].T


def settle(ref, sends, recvs):
    pltpu.make_async_copy(ref, ref, recvs).wait()
    pltpu.make_async_copy(ref, ref, sends).wait()


def over_z(z, y, sent, got, sends, recvs):
    def one(turn, carry):
        peer = lax.rem(z + turn, ALONG_Z)
        pltpu.make_async_remote_copy(
            src_ref=sent.at[pl.ds(pl.multiple_of(peer * SUB, SUB), SUB), :],
            dst_ref=got.at[pl.ds(pl.multiple_of(z * SUB, SUB), SUB), :],
            send_sem=sends,
            recv_sem=recvs,
            device_id={"gx": peer * ALONG_Y + y},
            device_id_type=MESH,
        ).start()
        return carry

    lax.fori_loop(1, ALONG_Z, one, 0)
    own = pl.ds(pl.multiple_of(z * SUB, SUB), SUB)
    got[own, :] = sent[own, :]
    settle(got.at[0 : (ALONG_Z - 1) * SUB], sends, recvs)


def over_y(z, y, sent, got, sends, recvs):
    for turn in range(1, ALONG_Y):
        peer = lax.rem(y + turn, ALONG_Y)
        pltpu.make_async_remote_copy(
            src_ref=sent.at[peer],
            dst_ref=got.at[y],
            send_sem=sends,
            recv_sem=recvs,
            device_id={"gx": z * ALONG_Y + peer},
            device_id_type=MESH,
        ).start()
    got[y] = sent[y]
    settle(got.at[0 : ALONG_Y - 1], sends, recvs)


def by_row(square, quarters):
    for y in range(ALONG_Y):
        for h in range(2):
            quarters[y, h * ALONG_Z : (h + 1) * ALONG_Z, :] = square[
                pl.ds(2 * y + h, ALONG_Z, stride=SUB), :
            ]


def by_tile(quarters, square):
    for y in range(ALONG_Y):
        for h in range(2):
            square[pl.ds(2 * y + h, ALONG_Z, stride=SUB), :] = quarters[
                y, h * ALONG_Z : (h + 1) * ALONG_Z, :
            ]


def whole_kernel(
    flow_in,
    residual_in,
    speeds_in,
    dissip_in,
    to_in,
    from_in,
    out_ref,
    flow,
    residual,
    speeds,
    dissip,
    to_modes,
    from_modes,
    kept,
    scale,
    rows,
    square,
    pack,
    edge_sent,
    edge_got,
    z_sent,
    z_got,
    y_sent,
    y_got,
    local_sem,
    halo_send,
    halo_recv,
    sends,
    recvs,
):
    gx = lax.axis_index("gx")
    gy = lax.axis_index("gy")
    z = lax.div(gx, ALONG_Y)
    y = lax.rem(gx, ALONG_Y)
    has_up, has_down = gx > 0, gx < GX - 1
    has_left, has_right = gy > 0, gy < GY - 1

    barrier = pltpu.get_barrier_semaphore()

    def greet_z(turn, carry):
        peer = lax.rem(z + turn, ALONG_Z) * ALONG_Y + y
        pl.semaphore_signal(barrier, 1, device_id={"gx": peer}, device_id_type=MESH)
        return carry

    lax.fori_loop(1, ALONG_Z, greet_z, 0)
    for turn in range(1, ALONG_Y):
        peer = z * ALONG_Y + lax.rem(y + turn, ALONG_Y)
        pl.semaphore_signal(barrier, 1, device_id={"gx": peer}, device_id_type=MESH)
    for there, axis, peer in (
        (has_up, "gx", gx - 1),
        (has_down, "gx", gx + 1),
        (has_left, "gy", gy - 1),
        (has_right, "gy", gy + 1),
    ):

        @pl.when(there)
        def _(axis=axis, peer=peer):
            pl.semaphore_signal(barrier, 1, device_id={axis: peer}, device_id_type=MESH)

    inner = flow.at[:, LEAD : LEAD + ROWS, :]
    loads = [
        pltpu.make_async_copy(a, b, local_sem.at[i])
        for i, (a, b) in enumerate(
            (
                (speeds_in, speeds),
                (dissip_in, dissip),
                (flow_in, inner),
                (residual_in, residual),
                (to_in, to_modes),
                (from_in, from_modes),
            )
        )
    ]
    for load in loads:
        load.start()

    @pl.when(jnp.logical_not(has_up))
    def _():
        flow[:, 0:LEAD, :] = jnp.zeros((FIELDS, LEAD, LANES), jnp.float32)

    @pl.when(jnp.logical_not(has_down))
    def _():
        flow[:, LEAD + ROWS :, :] = jnp.zeros((FIELDS, LEAD, LANES), jnp.float32)

    @pl.when(jnp.logical_not(has_left))
    def _():
        edge_got[0] = jnp.zeros((EDGES, LANES), jnp.float32)

    @pl.when(jnp.logical_not(has_right))
    def _():
        edge_got[1] = jnp.zeros((EDGES, LANES), jnp.float32)

    for load in loads:
        load.wait()
    pack_edges(flow, square, edge_sent)
    factor(speeds, dissip, kept, scale)

    near = (
        has_up.astype(jnp.int32)
        + has_down.astype(jnp.int32)
        + has_left.astype(jnp.int32)
        + has_right.astype(jnp.int32)
    )
    pl.semaphore_wait(barrier, ALONG_Z - 1 + ALONG_Y - 1 + near)

    def halo(i, src, dst, target):
        return pltpu.make_async_remote_copy(
            src_ref=src,
            dst_ref=dst,
            send_sem=halo_send.at[i],
            recv_sem=halo_recv.at[i],
            device_id=target,
            device_id_type=MESH,
        )

    below = halo(0, flow_in.at[:, ROWS - LEAD :, :], flow.at[:, 0:LEAD, :], {"gx": gx + 1})
    above = halo(1, flow_in.at[:, 0:LEAD, :], flow.at[:, LEAD + ROWS :, :], {"gx": gx - 1})
    right = halo(2, edge_sent, edge_got.at[0], {"gy": gy + 1})
    left = halo(3, edge_sent, edge_got.at[1], {"gy": gy - 1})
    pairs = (
        (below, has_down, has_up),
        (above, has_up, has_down),
        (right, has_right, has_left),
        (left, has_left, has_right),
    )
    for copy, sending, _ in pairs:
        pl.when(sending)(copy.start)
    for copy, sending, receiving in pairs:
        pl.when(receiving)(copy.wait_recv)
        pl.when(sending)(copy.wait_send)

    unpack_edges(edge_got, square)
    sweep(flow, square, residual, dissip, to_modes, kept, scale)
    condense(kept, rows, pack)
    z_sent[0] = pack[...].T
    over_z(z, y, z_sent.at[0], z_got.at[0], sends.at[0], recvs.at[0])
    by_row(z_got.at[0], y_sent.at[0])
    over_y(z, y, y_sent.at[0], y_got.at[0], sends.at[1], recvs.at[1])
    by_tile(y_got.at[0], square)
    pack[...] = square[...].T
    solve_ends(pack, square)
    pack[...] = square[...].T
    by_row(pack, y_sent.at[1])
    over_y(z, y, y_sent.at[1], y_got.at[1], sends.at[2], recvs.at[2])
    by_tile(y_got.at[1], z_sent.at[1])
    over_z(z, y, z_sent.at[1], z_got.at[1], sends.at[3], recvs.at[3])
    square[...] = z_got[1].T
    restore(square, kept, rows, from_modes, out_ref)


def local(flow_state, residual, speeds, dissip, to_modes, from_modes):
    f32 = jnp.float32
    block = (FIELDS, ROWS, LANES)
    quarters = (2, ALONG_Y, 2 * ALONG_Z, LANES)
    return pl.pallas_call(
        whole_kernel,
        out_shape=jax.ShapeDtypeStruct(block, f32),
        in_specs=[pl.BlockSpec(memory_space=pl.ANY)] * 6,
        out_specs=pl.BlockSpec(memory_space=pltpu.VMEM),
        scratch_shapes=[
            pltpu.VMEM((FIELDS, ROWS + 2 * LEAD, LANES), f32),
            pltpu.VMEM(block, f32),
            pltpu.VMEM(block, f32),
            pltpu.VMEM((ROWS, LANES), f32),
            pltpu.VMEM((FIELDS, FIELDS, LANES), f32),
            pltpu.VMEM((FIELDS, FIELDS, LANES), f32),
            pltpu.VMEM((FIELDS, STEPS, 5, SUB, LANES), f32),
            pltpu.VMEM((FIELDS, STEPS, 2, SUB, LANES), f32),
            pltpu.VMEM((FIELDS, 10, SUB, LANES), f32),
            pltpu.VMEM((LANES, LANES), f32),
            pltpu.VMEM((LANES, LANES), f32),
            pltpu.VMEM((EDGES, LANES), f32),
            pltpu.VMEM((2, EDGES, LANES), f32),
            pltpu.VMEM((2, LANES, LANES), f32),
            pltpu.VMEM((2, LANES, LANES), f32),
            pltpu.VMEM(quarters, f32),
            pltpu.VMEM(quarters, f32),
            pltpu.SemaphoreType.DMA((6,)),
            pltpu.SemaphoreType.DMA((4,)),
            pltpu.SemaphoreType.DMA((4,)),
            pltpu.SemaphoreType.DMA((4,)),
            pltpu.SemaphoreType.DMA((4,)),
        ],
        compiler_params=pltpu.CompilerParams(collective_id=0, has_side_effects=True),
    )(flow_state[0], residual[0], speeds[0], dissip[0], to_modes, from_modes)[None]


def solution(mesh):
    placed = (
        P(None, None, "gx", "gy"),
        P(None, None, "gx", "gy"),
        P(None, None, "gx", "gy"),
        P(None, "gx", "gy"),
        P(None, None, "gy"),
        P(None, None, "gy"),
    )
    return jax.shard_map(
        local, mesh=mesh, in_specs=placed, out_specs=P(None, None, "gx", "gy"), check_vma=False
    )
```

```python
import jax
import jax.numpy as jnp
from jax import lax
from jax.experimental import pallas as pl
from jax.experimental.pallas import tpu as pltpu
from jax.sharding import PartitionSpec as P

explicit_gain = 4.0
wide_share = 0.5
FIELDS = 5
ROWS = 128
LANES = 128
SUB = 8
STEPS = ROWS // SUB
LEAD = 8
SLOT = 24
BACK = 4


def mm(a, b):
    return tuple(
        tuple(a[i][0] * b[0][j] + a[i][1] * b[1][j] for j in range(2)) for i in range(2)
    )


def mv(a, v):
    return tuple(a[i][0] * v[0] + a[i][1] * v[1] for i in range(2))


def msub(a, b):
    return tuple(tuple(a[i][j] - b[i][j] for j in range(2)) for i in range(2))


def mneg(a):
    return tuple(tuple(-a[i][j] for j in range(2)) for i in range(2))


def vsub(a, b):
    return tuple(a[i] - b[i] for i in range(2))


def inverse_of_unit_less(a):
    upper = 1.0 - a[0][0]
    lower = 1.0 - a[1][1]
    scale = 1.0 / (upper * lower - a[0][1] * a[1][0])
    return ((lower * scale, a[0][1] * scale), (a[1][0] * scale, upper * scale))


def madd(a, b):
    return tuple(tuple(a[i][j] + b[i][j] for j in range(2)) for i in range(2))


def tree(fn, *items):
    return jax.tree.map(fn, *items)


def assemble(bottom, top_next):
    beta, c_mat, d_mat = bottom
    p_next, a_next, b_next = top_next
    solver = inverse_of_unit_less(mm(d_mat, a_next))
    return (
        mv(solver, vsub(beta, mv(d_mat, p_next))),
        mm(solver, c_mat),
        mneg(mm(solver, mm(d_mat, b_next))),
    )


def reduce_row(row, left, right):
    r, l_mat, r_mat = row
    solver = inverse_of_unit_less(madd(mm(l_mat, left[2]), mm(r_mat, right[1])))
    return (
        mv(solver, vsub(vsub(r, mv(l_mat, left[0])), mv(r_mat, right[0]))),
        mneg(mm(solver, mm(l_mat, left[1]))),
        mneg(mm(solver, mm(r_mat, right[2]))),
    )


def spread(row):
    return jnp.broadcast_to(row, (SUB, LANES))


def strided(ref, f, start):
    return ref[f, pl.ds(start, SUB, stride=STEPS), :]


def forcing_of(flow_ref, edge, residual_ref, damp, f, j, lane):
    mid = strided(flow_ref, f, LEAD + j)
    stream = (
        strided(flow_ref, f, LEAD + j - 2)
        - 4.0 * strided(flow_ref, f, LEAD + j - 1)
        + 6.0 * mid
        - 4.0 * strided(flow_ref, f, LEAD + j + 1)
        + strided(flow_ref, f, LEAD + j + 2)
    )
    back_two = jnp.where(lane < 2, edge, pltpu.roll(mid, 2, 1))
    back_one = jnp.where(lane < 1, pltpu.roll(edge, LANES - 1, 1), pltpu.roll(mid, 1, 1))
    next_one = jnp.where(lane >= LANES - 1, pltpu.roll(edge, 1, 1), pltpu.roll(mid, LANES - 1, 1))
    next_two = jnp.where(lane >= LANES - 2, edge, pltpu.roll(mid, LANES - 2, 1))
    cross = back_two - 4.0 * back_one + 6.0 * mid - 4.0 * next_one + next_two
    return strided(residual_ref, f, j) - explicit_gain * damp * (stream + cross)


def factor(steps, state, speeds_ref, dissip_ref, kept_ref, scale_ref):
    zero = jnp.zeros((SUB, LANES), jnp.float32)
    minus = zero - 1.0
    if state is None:
        state = (
            [(zero, zero, minus, zero) for _ in range(FIELDS)],
            [(zero, zero, zero, minus) for _ in range(FIELDS)],
        )
    old, last = state
    for j in steps:
        damp = dissip_ref[pl.ds(j, SUB, stride=STEPS), :]
        for f in range(FIELDS):
            speed = strided(speeds_ref, f, j)
            magnitude = jnp.abs(speed)
            near = damp * magnitude
            far = wide_share * near
            near_low = -(jnp.maximum(speed, 0.0) + near)
            centre = 1.0 + magnitude + 2.0 * near + 2.0 * far
            near_up = -(jnp.maximum(-speed, 0.0) + near)
            outer = -far
            reduced = near_low - outer * old[f][0]
            leading = centre - outer * old[f][1]
            pivot_inv = 1.0 / (leading - reduced * last[f][0])
            upper_two = outer * pivot_inv
            low = reduced * pivot_inv
            now = (
                (near_up - reduced * last[f][1]) * pivot_inv,
                upper_two,
                -(upper_two * old[f][2] + low * last[f][2]),
                -(upper_two * old[f][3] + low * last[f][3]),
            )
            for q in range(4):
                kept_ref[f, j, q] = now[q]
            scale_ref[f, j, 0] = pivot_inv
            scale_ref[f, j, 1] = low
            old[f], last[f] = last[f], now
    return old, last


def sweep(flow_ref, edge_ref, residual_ref, dissip_ref, to_ref, kept_ref, scale_ref):
    lane = lax.broadcasted_iota(jnp.int32, (SUB, LANES), 1)
    zero = jnp.zeros((SUB, LANES), jnp.float32)
    old = [zero] * FIELDS
    last = [zero] * FIELDS
    for j in range(STEPS):
        damp = dissip_ref[pl.ds(j, SUB, stride=STEPS), :]
        edges = edge_ref[pl.ds(j, SUB, stride=STEPS), :]
        forcing = [
            forcing_of(
                flow_ref,
                pltpu.roll(edges, LANES - 2 - SUB * f, 1),
                residual_ref,
                damp,
                f,
                j,
                lane,
            )
            for f in range(FIELDS)
        ]
        for f in range(FIELDS):
            modal = spread(to_ref[f, 0:1, :]) * forcing[0]
            for k in range(1, FIELDS):
                modal = modal + spread(to_ref[f, k : k + 1, :]) * forcing[k]
            now = (
                modal * scale_ref[f, j, 0]
                - kept_ref[f, j, 1] * old[f]
                - scale_ref[f, j, 1] * last[f]
            )
            kept_ref[f, j, 4] = now
            old[f], last[f] = last[f], now


def condense(kept_ref, rows_ref, pack_ref):
    sub = lax.broadcasted_iota(jnp.int32, (SUB, LANES), 0)
    zero = jnp.zeros((SUB, LANES), jnp.float32)
    minus = zero - 1.0
    none_vec = (zero, zero)
    none_mat = ((zero, zero), (zero, zero))
    minus_eye = ((minus, zero), (zero, minus))
    at_left = (none_vec, minus_eye, none_mat)
    at_right = (none_vec, none_mat, minus_eye)
    pack_ref[...] = jnp.zeros((LANES, LANES), jnp.float32)
    for f in range(FIELDS):
        u1a, u2a, z1a, z2a, ya = (kept_ref[f, STEPS - 2, q] for q in range(5))
        u1b, u2b, z1b, z2b, yb = (kept_ref[f, STEPS - 1, q] for q in range(5))
        beta = (ya - u1a * yb, yb)
        c_mat = ((z1a - u1a * z1b, z2a - u1a * z2b), (z1b, z2b))
        d_mat = ((u2a - u1a * u1b, -u1a * u2b), (u1b, u2b))
        nearer = (zero, zero, zero, minus, zero)
        farther = (zero, zero, zero, zero, minus)
        for j in reversed(range(STEPS - 2)):
            one = kept_ref[f, j, 0]
            two = kept_ref[f, j, 1]
            own = (kept_ref[f, j, 4], kept_ref[f, j, 2], kept_ref[f, j, 3])
            current = tuple(
                own[q] - one * nearer[q] - two * farther[q] for q in range(3)
            ) + tuple(-(one * nearer[q] + two * farther[q]) for q in range(3, 5))
            nearer, farther = current, nearer
        p_vec = (nearer[0], farther[0])
        a_mat = ((nearer[1], nearer[2]), (farther[1], farther[2]))
        b_mat = ((nearer[3], nearer[4]), (farther[3], farther[4]))
        top_next = tree(lambda a: pltpu.roll(a, SUB - 1, 0), (p_vec, a_mat, b_mat))
        row = assemble((beta, c_mat, d_mat), top_next)
        row = tree(lambda a, e: jnp.where(sub == SUB - 1, e, a), row, at_right)
        for step in (1, 2, 4):
            left = tree(lambda a, e: jnp.where(sub < step, e, pltpu.roll(a, step, 0)), row, at_left)
            right = tree(
                lambda a, e: jnp.where(sub >= SUB - 1 - step, e, pltpu.roll(a, SUB - step, 0)),
                row,
                at_right,
            )
            row = reduce_row(row, left, right)
        for q, a in enumerate(jax.tree.leaves(row)):
            rows_ref[f, q] = a
        top = (
            vsub(p_vec, mv(b_mat, row[0])),
            msub(a_mat, mm(b_mat, row[1])),
            mneg(mm(b_mat, row[2])),
        )
        before = tree(lambda a: pltpu.roll(a, 1, 0), row)
        solver = inverse_of_unit_less(mm(c_mat, before[2]))
        bottom = (
            mv(solver, vsub(beta, mv(c_mat, before[0]))),
            mneg(mm(solver, mm(c_mat, before[1]))),
            mm(solver, d_mat),
        )
        for q, a in enumerate(jax.tree.leaves(top)):
            pack_ref[f * SLOT + q : f * SLOT + q + 1, :] = a[0:1]
        for q, a in enumerate(jax.tree.leaves(bottom)):
            pack_ref[f * SLOT + 10 + q : f * SLOT + 11 + q, :] = a[SUB - 1 : SUB]


def as_relation(leaves):
    return (
        (leaves[0], leaves[1]),
        ((leaves[2], leaves[3]), (leaves[4], leaves[5])),
        ((leaves[6], leaves[7]), (leaves[8], leaves[9])),
    )


def solve_ends(pack_ref, back_ref):
    leaves = [pack_ref[pl.ds(q, FIELDS, stride=SLOT), :] for q in range(20)]
    lane = lax.broadcasted_iota(jnp.int32, (FIELDS, LANES), 1)
    top = as_relation(leaves[:10])
    bottom = as_relation(leaves[10:])
    top_next = tree(lambda a: jnp.where(lane >= LANES - 2, 0.0, pltpu.roll(a, LANES - 2, 1)), top)
    row = assemble(bottom, top_next)
    step = 2
    while step < LANES:
        left = tree(lambda a: jnp.where(lane < step, 0.0, pltpu.roll(a, step, 1)), row)
        right = tree(
            lambda a: jnp.where(lane >= LANES - step, 0.0, pltpu.roll(a, LANES - step, 1)), row
        )
        row = reduce_row(row, left, right)
        step *= 2
    own = row[0]
    behind = tree(lambda a: jnp.where(lane < 2, 0.0, pltpu.roll(a, 2, 1)), own)
    back_ref[...] = jnp.zeros((LANES, LANES), jnp.float32)
    for v, a in enumerate(behind + own):
        for f in range(FIELDS):
            back_ref[f * BACK + v : f * BACK + v + 1, :] = a[f : f + 1]


def restore(ends_ref, kept_ref, rows_ref, from_ref, out_ref):
    sub = lax.broadcasted_iota(jnp.int32, (SUB, LANES), 0)
    behind, state = [], []
    for f in range(FIELDS):
        edge = [spread(ends_ref[f * BACK + v : f * BACK + v + 1, :]) for v in range(BACK)]
        row = as_relation([rows_ref[f, q] for q in range(10)])
        cut = vsub(vsub(row[0], mv(row[1], edge[:2])), mv(row[2], edge[2:]))
        behind.append(
            tuple(jnp.where(sub == 0, edge[v], pltpu.roll(cut[v], 1, 0)) for v in range(2))
        )
        state.append(cut)
    for j in reversed(range(STEPS)):
        update = []
        for f in range(FIELDS):
            if j >= STEPS - 2:
                update.append(state[f][j - (STEPS - 2)])
                continue
            nearer, farther = state[f]
            current = (
                kept_ref[f, j, 4]
                - kept_ref[f, j, 2] * behind[f][0]
                - kept_ref[f, j, 3] * behind[f][1]
                - kept_ref[f, j, 1] * farther
                - kept_ref[f, j, 0] * nearer
            )
            state[f] = (current, nearer)
            update.append(current)
        for k in range(FIELDS):
            total = spread(from_ref[k, 0:1, :]) * update[0]
            for m in range(1, FIELDS):
                total = total + spread(from_ref[k, m : m + 1, :]) * update[m]
            out_ref[k, pl.ds(j, SUB, stride=STEPS), :] = total


ALONG_Y = 4
ALONG_Z = 16
GX = ALONG_Y * ALONG_Z
GY = 8
MESH = pl.DeviceIdType.MESH
EDGES = FIELDS * SUB


def pack_edges(flow_ref, square_ref, sent_ref):
    lane = lax.broadcasted_iota(jnp.int32, (ROWS, LANES), 1)
    total = jnp.zeros((ROWS, LANES), jnp.float32)
    for f in range(FIELDS):
        mid = flow_ref[f, LEAD : LEAD + ROWS, :]
        at = lane - SUB * f
        total = jnp.where((at >= 0) & (at < 2), pltpu.roll(mid, SUB * f, 1) if f else mid, total)
        total = jnp.where((at >= 2) & (at < 4), pltpu.roll(mid, SUB * f + 4, 1), total)
    square_ref[...] = total.T
    sent_ref[...] = square_ref[0:EDGES, :]


def unpack_edges(got_ref, square_ref):
    row = lax.broadcasted_iota(jnp.int32, (EDGES, LANES), 0)
    square_ref[...] = jnp.zeros((LANES, LANES), jnp.float32)
    square_ref[0:EDGES, :] = jnp.where(lax.rem(row, SUB) < 2, got_ref[1], got_ref[0])
    square_ref[...] = square_ref[...].T


def settle(ref, sends, recvs):
    pltpu.make_async_copy(ref, ref, recvs).wait()
    pltpu.make_async_copy(ref, ref, sends).wait()


def over_z(z, y, sent, got, sends, recvs):
    def one(turn, carry):
        peer = lax.rem(z + turn, ALONG_Z)
        pltpu.make_async_remote_copy(
            src_ref=sent.at[pl.ds(pl.multiple_of(peer * SUB, SUB), SUB), :],
            dst_ref=got.at[pl.ds(pl.multiple_of(z * SUB, SUB), SUB), :],
            send_sem=sends,
            recv_sem=recvs,
            device_id={"gx": peer * ALONG_Y + y},
            device_id_type=MESH,
        ).start()
        return carry

    lax.fori_loop(1, ALONG_Z, one, 0)
    own = pl.ds(pl.multiple_of(z * SUB, SUB), SUB)
    got[own, :] = sent[own, :]
    settle(got.at[0 : (ALONG_Z - 1) * SUB], sends, recvs)


def over_y(z, y, sent, got, sends, recvs):
    for turn in range(1, ALONG_Y):
        peer = lax.rem(y + turn, ALONG_Y)
        pltpu.make_async_remote_copy(
            src_ref=sent.at[peer],
            dst_ref=got.at[y],
            send_sem=sends,
            recv_sem=recvs,
            device_id={"gx": z * ALONG_Y + peer},
            device_id_type=MESH,
        ).start()
    got[y] = sent[y]
    settle(got.at[0 : ALONG_Y - 1], sends, recvs)


def by_row(square, quarters):
    for y in range(ALONG_Y):
        for h in range(2):
            quarters[y, h * ALONG_Z : (h + 1) * ALONG_Z, :] = square[
                pl.ds(2 * y + h, ALONG_Z, stride=SUB), :
            ]


def by_tile(quarters, square):
    for y in range(ALONG_Y):
        for h in range(2):
            square[pl.ds(2 * y + h, ALONG_Z, stride=SUB), :] = quarters[
                y, h * ALONG_Z : (h + 1) * ALONG_Z, :
            ]


def whole_kernel(
    flow_in,
    residual_in,
    speeds_in,
    dissip_in,
    to_in,
    from_in,
    ends_ref,
    kept,
    rows,
    from_modes,
    flow,
    residual,
    speeds,
    dissip,
    to_modes,
    scale,
    square,
    pack,
    edge_sent,
    edge_got,
    z_sent,
    z_got,
    y_sent,
    y_got,
    local_sem,
    halo_send,
    halo_recv,
    sends,
    recvs,
    relay,
):
    gx = lax.axis_index("gx")
    gy = lax.axis_index("gy")
    z = lax.div(gx, ALONG_Y)
    y = lax.rem(gx, ALONG_Y)
    has_up, has_down = gx > 0, gx < GX - 1
    has_left, has_right = gy > 0, gy < GY - 1

    barrier = pltpu.get_barrier_semaphore()

    def along_z(shift):
        return {"gx": lax.rem(z + ALONG_Z + shift, ALONG_Z) * ALONG_Y + y}

    def tell_z(semaphore, distance):
        for shift in (distance, -distance):
            pl.semaphore_signal(
                semaphore, 1, device_id=along_z(shift), device_id_type=MESH
            )

    tell_z(barrier, 1)
    for turn in range(1, ALONG_Y):
        peer = z * ALONG_Y + lax.rem(y + turn, ALONG_Y)
        pl.semaphore_signal(barrier, 1, device_id={"gx": peer}, device_id_type=MESH)
    for there, axis, peer in (
        (has_up, "gx", gx - 1),
        (has_down, "gx", gx + 1),
        (has_left, "gy", gy - 1),
        (has_right, "gy", gy + 1),
    ):

        @pl.when(there)
        def _(axis=axis, peer=peer):
            pl.semaphore_signal(barrier, 1, device_id={axis: peer}, device_id_type=MESH)

    inner = flow.at[:, LEAD : LEAD + ROWS, :]
    loads = [
        pltpu.make_async_copy(a, b, local_sem.at[i])
        for i, (a, b) in enumerate(
            (
                (speeds_in, speeds),
                (dissip_in, dissip),
                (flow_in, inner),
                (residual_in, residual),
                (to_in, to_modes),
                (from_in, from_modes),
            )
        )
    ]
    for load in loads:
        load.start()

    @pl.when(jnp.logical_not(has_up))
    def _():
        flow[:, 0:LEAD, :] = jnp.zeros((FIELDS, LEAD, LANES), jnp.float32)

    @pl.when(jnp.logical_not(has_down))
    def _():
        flow[:, LEAD + ROWS :, :] = jnp.zeros((FIELDS, LEAD, LANES), jnp.float32)

    @pl.when(jnp.logical_not(has_left))
    def _():
        edge_got[0] = jnp.zeros((EDGES, LANES), jnp.float32)

    @pl.when(jnp.logical_not(has_right))
    def _():
        edge_got[1] = jnp.zeros((EDGES, LANES), jnp.float32)

    for load in loads:
        load.wait()
    pack_edges(flow, square, edge_sent)

    near = (
        has_up.astype(jnp.int32)
        + has_down.astype(jnp.int32)
        + has_left.astype(jnp.int32)
        + has_right.astype(jnp.int32)
    )
    pl.semaphore_wait(barrier, 2 + ALONG_Y - 1 + near)

    def halo(i, src, dst, target):
        return pltpu.make_async_remote_copy(
            src_ref=src,
            dst_ref=dst,
            send_sem=halo_send.at[i],
            recv_sem=halo_recv.at[i],
            device_id=target,
            device_id_type=MESH,
        )

    below = halo(0, flow_in.at[:, ROWS - LEAD :, :], flow.at[:, 0:LEAD, :], {"gx": gx + 1})
    above = halo(1, flow_in.at[:, 0:LEAD, :], flow.at[:, LEAD + ROWS :, :], {"gx": gx - 1})
    right = halo(2, edge_sent, edge_got.at[0], {"gy": gy + 1})
    left = halo(3, edge_sent, edge_got.at[1], {"gy": gy - 1})
    pairs = (
        (below, has_down, has_up),
        (above, has_up, has_down),
        (right, has_right, has_left),
        (left, has_left, has_right),
    )
    for copy, sending, _ in pairs:
        pl.when(sending)(copy.start)

    tell_z(relay.at[0], 1)
    state = factor(range(STEPS // 2), None, speeds, dissip, kept, scale)
    pl.semaphore_wait(relay.at[0], 2)
    tell_z(relay.at[1], 2)
    factor(range(STEPS // 2, STEPS), state, speeds, dissip, kept, scale)
    pl.semaphore_wait(relay.at[1], 2)
    tell_z(relay.at[2], 4)

    for copy, sending, receiving in pairs:
        pl.when(receiving)(copy.wait_recv)
        pl.when(sending)(copy.wait_send)

    unpack_edges(edge_got, square)
    sweep(flow, square, residual, dissip, to_modes, kept, scale)
    condense(kept, rows, pack)
    z_sent[0] = pack[...].T
    pl.semaphore_wait(relay.at[2], 2)
    over_z(z, y, z_sent.at[0], z_got.at[0], sends.at[0], recvs.at[0])
    by_row(z_got.at[0], y_sent.at[0])
    over_y(z, y, y_sent.at[0], y_got.at[0], sends.at[1], recvs.at[1])
    by_tile(y_got.at[0], square)
    pack[...] = square[...].T
    solve_ends(pack, square)
    pack[...] = square[...].T
    by_row(pack, y_sent.at[1])
    over_y(z, y, y_sent.at[1], y_got.at[1], sends.at[2], recvs.at[2])
    by_tile(y_got.at[1], z_sent.at[1])
    over_z(z, y, z_sent.at[1], z_got.at[1], sends.at[3], recvs.at[3])
    ends_ref[...] = z_got[1].T


def last_kernel(ends, kept, rows, from_modes, out):
    restore(ends, kept, rows, from_modes, out)


def local(flow_state, residual, speeds, dissip, to_modes, from_modes):
    f32 = jnp.float32
    block = (FIELDS, ROWS, LANES)
    quarters = (2, ALONG_Y, 2 * ALONG_Z, LANES)
    vmem = pl.BlockSpec(memory_space=pltpu.VMEM)
    ends, kept, rows, modes_back = pl.pallas_call(
        whole_kernel,
        out_shape=(
            jax.ShapeDtypeStruct((LANES, LANES), f32),
            jax.ShapeDtypeStruct((FIELDS, STEPS, 5, SUB, LANES), f32),
            jax.ShapeDtypeStruct((FIELDS, 10, SUB, LANES), f32),
            jax.ShapeDtypeStruct((FIELDS, FIELDS, LANES), f32),
        ),
        in_specs=[pl.BlockSpec(memory_space=pltpu.HBM)] * 6,
        out_specs=(vmem,) * 4,
        scratch_shapes=[
            pltpu.VMEM((FIELDS, ROWS + 2 * LEAD, LANES), f32),
            pltpu.VMEM(block, f32),
            pltpu.VMEM(block, f32),
            pltpu.VMEM((ROWS, LANES), f32),
            pltpu.VMEM((FIELDS, FIELDS, LANES), f32),
            pltpu.VMEM((FIELDS, STEPS, 2, SUB, LANES), f32),
            pltpu.VMEM((LANES, LANES), f32),
            pltpu.VMEM((LANES, LANES), f32),
            pltpu.VMEM((EDGES, LANES), f32),
            pltpu.VMEM((2, EDGES, LANES), f32),
            pltpu.VMEM((2, LANES, LANES), f32),
            pltpu.VMEM((2, LANES, LANES), f32),
            pltpu.VMEM(quarters, f32),
            pltpu.VMEM(quarters, f32),
            pltpu.SemaphoreType.DMA((6,)),
            pltpu.SemaphoreType.DMA((4,)),
            pltpu.SemaphoreType.DMA((4,)),
            pltpu.SemaphoreType.DMA((4,)),
            pltpu.SemaphoreType.DMA((4,)),
            pltpu.SemaphoreType.REGULAR((3,)),
        ],
        compiler_params=pltpu.CompilerParams(
            collective_id=0, has_side_effects=True, vmem_limit_bytes=24 << 20
        ),
    )(
        *(
            pltpu.with_memory_space_constraint(a, pltpu.HBM)
            for a in (flow_state[0], residual[0], speeds[0], dissip[0], to_modes, from_modes)
        )
    )
    return pl.pallas_call(
        last_kernel,
        out_shape=jax.ShapeDtypeStruct(block, f32),
        in_specs=[vmem] * 4,
        out_specs=vmem,
        compiler_params=pltpu.CompilerParams(vmem_limit_bytes=24 << 20),
    )(ends, kept, rows, modes_back)[None]


def solution(mesh):
    placed = (
        P(None, None, "gx", "gy"),
        P(None, None, "gx", "gy"),
        P(None, None, "gx", "gy"),
        P(None, "gx", "gy"),
        P(None, None, "gy"),
        P(None, None, "gy"),
    )
    return jax.shard_map(
        local, mesh=mesh, in_specs=placed, out_specs=P(None, None, "gx", "gy"), check_vma=False
    )
```

```python
import jax
import jax.numpy as jnp
from jax import lax
from jax.experimental import pallas as pl
from jax.experimental.pallas import tpu as pltpu
from jax.sharding import PartitionSpec as P

explicit_gain = 4.0
wide_share = 0.5
FIELDS = 5
ROWS = 128
LANES = 128
SUB = 8
STEPS = ROWS // SUB
LEAD = 8
SLOT = 24
BACK = 4
ALONG_Y = 4
ALONG_Z = 16
GX = ALONG_Y * ALONG_Z
GY = 8
MESH = pl.DeviceIdType.MESH
EDGES = FIELDS * SUB


def mm(a, b):
    return tuple(
        tuple(a[i][0] * b[0][j] + a[i][1] * b[1][j] for j in range(2)) for i in range(2)
    )


def mv(a, v):
    return tuple(a[i][0] * v[0] + a[i][1] * v[1] for i in range(2))


def msub(a, b):
    return tuple(tuple(a[i][j] - b[i][j] for j in range(2)) for i in range(2))


def mneg(a):
    return tuple(tuple(-a[i][j] for j in range(2)) for i in range(2))


def vsub(a, b):
    return tuple(a[i] - b[i] for i in range(2))


def inverse_of_unit_less(a):
    upper = 1.0 - a[0][0]
    lower = 1.0 - a[1][1]
    scale = 1.0 / (upper * lower - a[0][1] * a[1][0])
    return ((lower * scale, a[0][1] * scale), (a[1][0] * scale, upper * scale))


def madd(a, b):
    return tuple(tuple(a[i][j] + b[i][j] for j in range(2)) for i in range(2))


def tree(fn, *items):
    return jax.tree.map(fn, *items)


def assemble(bottom, top_next):
    beta, c_mat, d_mat = bottom
    p_next, a_next, b_next = top_next
    solver = inverse_of_unit_less(mm(d_mat, a_next))
    return (
        mv(solver, vsub(beta, mv(d_mat, p_next))),
        mm(solver, c_mat),
        mneg(mm(solver, mm(d_mat, b_next))),
    )


def reduce_row(row, left, right):
    r, l_mat, r_mat = row
    solver = inverse_of_unit_less(madd(mm(l_mat, left[2]), mm(r_mat, right[1])))
    return (
        mv(solver, vsub(vsub(r, mv(l_mat, left[0])), mv(r_mat, right[0]))),
        mneg(mm(solver, mm(l_mat, left[1]))),
        mneg(mm(solver, mm(r_mat, right[2]))),
    )


def spread(row):
    return jnp.broadcast_to(row, (SUB, LANES))


def strided(ref, f, start):
    return ref[f, pl.ds(start, SUB, stride=STEPS), :]


def forcing_of(flow_ref, edge, residual_ref, damp, f, j, lane):
    mid = strided(flow_ref, f, LEAD + j)
    stream = (
        strided(flow_ref, f, LEAD + j - 2)
        - 4.0 * strided(flow_ref, f, LEAD + j - 1)
        + 6.0 * mid
        - 4.0 * strided(flow_ref, f, LEAD + j + 1)
        + strided(flow_ref, f, LEAD + j + 2)
    )
    back_two = jnp.where(lane < 2, edge, pltpu.roll(mid, 2, 1))
    back_one = jnp.where(lane < 1, pltpu.roll(edge, LANES - 1, 1), pltpu.roll(mid, 1, 1))
    next_one = jnp.where(lane >= LANES - 1, pltpu.roll(edge, 1, 1), pltpu.roll(mid, LANES - 1, 1))
    next_two = jnp.where(lane >= LANES - 2, edge, pltpu.roll(mid, LANES - 2, 1))
    cross = back_two - 4.0 * back_one + 6.0 * mid - 4.0 * next_one + next_two
    return strided(residual_ref, f, j) - explicit_gain * damp * (stream + cross)


def factor(steps, state, speeds_ref, dissip_ref, kept_ref, scale_ref):
    zero = jnp.zeros((SUB, LANES), jnp.float32)
    minus = zero - 1.0
    if state is None:
        state = (
            [(zero, zero, minus, zero) for _ in range(FIELDS)],
            [(zero, zero, zero, minus) for _ in range(FIELDS)],
        )
    old, last = state
    for j in steps:
        damp = dissip_ref[pl.ds(j, SUB, stride=STEPS), :]
        for f in range(FIELDS):
            speed = strided(speeds_ref, f, j)
            magnitude = jnp.abs(speed)
            near = damp * magnitude
            far = wide_share * near
            near_low = -(jnp.maximum(speed, 0.0) + near)
            centre = 1.0 + magnitude + 2.0 * near + 2.0 * far
            near_up = -(jnp.maximum(-speed, 0.0) + near)
            outer = -far
            reduced = near_low - outer * old[f][0]
            leading = centre - outer * old[f][1]
            pivot_inv = 1.0 / (leading - reduced * last[f][0])
            upper_two = outer * pivot_inv
            low = reduced * pivot_inv
            now = (
                (near_up - reduced * last[f][1]) * pivot_inv,
                upper_two,
                -(upper_two * old[f][2] + low * last[f][2]),
                -(upper_two * old[f][3] + low * last[f][3]),
            )
            for q in range(4):
                kept_ref[f, j, q] = now[q]
            scale_ref[f, j, 0] = pivot_inv
            scale_ref[f, j, 1] = low
            old[f], last[f] = last[f], now
    return old, last


def sweep(flow_ref, edge_ref, residual_ref, dissip_ref, to_ref, kept_ref, scale_ref):
    lane = lax.broadcasted_iota(jnp.int32, (SUB, LANES), 1)
    zero = jnp.zeros((SUB, LANES), jnp.float32)
    old = [zero] * FIELDS
    last = [zero] * FIELDS
    for j in range(STEPS):
        damp = dissip_ref[pl.ds(j, SUB, stride=STEPS), :]
        edges = edge_ref[pl.ds(j, SUB, stride=STEPS), :]
        forcing = [
            forcing_of(
                flow_ref,
                pltpu.roll(edges, LANES - 2 - SUB * f, 1),
                residual_ref,
                damp,
                f,
                j,
                lane,
            )
            for f in range(FIELDS)
        ]
        for f in range(FIELDS):
            modal = spread(to_ref[f, 0:1, :]) * forcing[0]
            for k in range(1, FIELDS):
                modal = modal + spread(to_ref[f, k : k + 1, :]) * forcing[k]
            now = (
                modal * scale_ref[f, j, 0]
                - kept_ref[f, j, 1] * old[f]
                - scale_ref[f, j, 1] * last[f]
            )
            kept_ref[f, j, 4] = now
            old[f], last[f] = last[f], now


def condense(kept_ref, rows_ref, pack_ref):
    sub = lax.broadcasted_iota(jnp.int32, (SUB, LANES), 0)
    zero = jnp.zeros((SUB, LANES), jnp.float32)
    minus = zero - 1.0
    none_vec = (zero, zero)
    none_mat = ((zero, zero), (zero, zero))
    minus_eye = ((minus, zero), (zero, minus))
    at_left = (none_vec, minus_eye, none_mat)
    at_right = (none_vec, none_mat, minus_eye)
    pack_ref[...] = jnp.zeros((LANES, LANES), jnp.float32)
    for f in range(FIELDS):
        u1a, u2a, z1a, z2a, ya = (kept_ref[f, STEPS - 2, q] for q in range(5))
        u1b, u2b, z1b, z2b, yb = (kept_ref[f, STEPS - 1, q] for q in range(5))
        beta = (ya - u1a * yb, yb)
        c_mat = ((z1a - u1a * z1b, z2a - u1a * z2b), (z1b, z2b))
        d_mat = ((u2a - u1a * u1b, -u1a * u2b), (u1b, u2b))
        nearer = (zero, zero, zero, minus, zero)
        farther = (zero, zero, zero, zero, minus)
        for j in reversed(range(STEPS - 2)):
            one = kept_ref[f, j, 0]
            two = kept_ref[f, j, 1]
            own = (kept_ref[f, j, 4], kept_ref[f, j, 2], kept_ref[f, j, 3])
            current = tuple(
                own[q] - one * nearer[q] - two * farther[q] for q in range(3)
            ) + tuple(-(one * nearer[q] + two * farther[q]) for q in range(3, 5))
            nearer, farther = current, nearer
        p_vec = (nearer[0], farther[0])
        a_mat = ((nearer[1], nearer[2]), (farther[1], farther[2]))
        b_mat = ((nearer[3], nearer[4]), (farther[3], farther[4]))
        top_next = tree(lambda a: pltpu.roll(a, SUB - 1, 0), (p_vec, a_mat, b_mat))
        row = assemble((beta, c_mat, d_mat), top_next)
        row = tree(lambda a, e: jnp.where(sub == SUB - 1, e, a), row, at_right)
        for step in (1, 2, 4):
            left = tree(lambda a, e: jnp.where(sub < step, e, pltpu.roll(a, step, 0)), row, at_left)
            right = tree(
                lambda a, e: jnp.where(sub >= SUB - 1 - step, e, pltpu.roll(a, SUB - step, 0)),
                row,
                at_right,
            )
            row = reduce_row(row, left, right)
        for q, a in enumerate(jax.tree.leaves(row)):
            rows_ref[f, q] = a
        top = (
            vsub(p_vec, mv(b_mat, row[0])),
            msub(a_mat, mm(b_mat, row[1])),
            mneg(mm(b_mat, row[2])),
        )
        before = tree(lambda a: pltpu.roll(a, 1, 0), row)
        solver = inverse_of_unit_less(mm(c_mat, before[2]))
        bottom = (
            mv(solver, vsub(beta, mv(c_mat, before[0]))),
            mneg(mm(solver, mm(c_mat, before[1]))),
            mm(solver, d_mat),
        )
        for q, a in enumerate(jax.tree.leaves(top)):
            pack_ref[f * SLOT + q : f * SLOT + q + 1, :] = a[0:1]
        for q, a in enumerate(jax.tree.leaves(bottom)):
            pack_ref[f * SLOT + 10 + q : f * SLOT + 11 + q, :] = a[SUB - 1 : SUB]


def as_relation(leaves):
    return (
        (leaves[0], leaves[1]),
        ((leaves[2], leaves[3]), (leaves[4], leaves[5])),
        ((leaves[6], leaves[7]), (leaves[8], leaves[9])),
    )


def solve_ends(pack_ref, back_ref):
    leaves = [pack_ref[pl.ds(q, FIELDS, stride=SLOT), :] for q in range(20)]
    place = lax.rem(lax.broadcasted_iota(jnp.int32, (FIELDS, LANES), 1), GX)

    def earlier(item, step):
        return tree(lambda a: jnp.where(place < step, 0.0, pltpu.roll(a, step, 1)), item)

    def later(item, step):
        return tree(
            lambda a: jnp.where(place >= GX - step, 0.0, pltpu.roll(a, LANES - step, 1)), item
        )

    row = assemble(as_relation(leaves[10:]), later(as_relation(leaves[:10]), 1))
    for step in (1, 2, 4, 8, 16, 32):
        row = reduce_row(row, earlier(row, step), later(row, step))
    own = row[0]
    back_ref[...] = jnp.zeros((LANES, LANES), jnp.float32)
    for v, a in enumerate(earlier(own, 1) + own):
        for f in range(FIELDS):
            back_ref[f * BACK + v : f * BACK + v + 1, :] = a[f : f + 1]


def restore(ends_ref, kept_ref, rows_ref, from_ref, out_ref):
    sub = lax.broadcasted_iota(jnp.int32, (SUB, LANES), 0)
    behind, state = [], []
    for f in range(FIELDS):
        edge = [spread(ends_ref[f * BACK + v : f * BACK + v + 1, :]) for v in range(BACK)]
        row = as_relation([rows_ref[f, q] for q in range(10)])
        cut = vsub(vsub(row[0], mv(row[1], edge[:2])), mv(row[2], edge[2:]))
        behind.append(
            tuple(jnp.where(sub == 0, edge[v], pltpu.roll(cut[v], 1, 0)) for v in range(2))
        )
        state.append(cut)
    for j in reversed(range(STEPS)):
        update = []
        for f in range(FIELDS):
            if j >= STEPS - 2:
                update.append(state[f][j - (STEPS - 2)])
                continue
            nearer, farther = state[f]
            current = (
                kept_ref[f, j, 4]
                - kept_ref[f, j, 2] * behind[f][0]
                - kept_ref[f, j, 3] * behind[f][1]
                - kept_ref[f, j, 1] * farther
                - kept_ref[f, j, 0] * nearer
            )
            state[f] = (current, nearer)
            update.append(current)
        for k in range(FIELDS):
            total = spread(from_ref[k, 0:1, :]) * update[0]
            for m in range(1, FIELDS):
                total = total + spread(from_ref[k, m : m + 1, :]) * update[m]
            out_ref[k, pl.ds(j, SUB, stride=STEPS), :] = total


def pack_edges(flow_ref, square_ref, sent_ref):
    lane = lax.broadcasted_iota(jnp.int32, (ROWS, LANES), 1)
    total = jnp.zeros((ROWS, LANES), jnp.float32)
    for f in range(FIELDS):
        mid = flow_ref[f, LEAD : LEAD + ROWS, :]
        at = lane - SUB * f
        total = jnp.where((at >= 0) & (at < 2), pltpu.roll(mid, SUB * f, 1) if f else mid, total)
        total = jnp.where((at >= 2) & (at < 4), pltpu.roll(mid, SUB * f + 4, 1), total)
    square_ref[...] = total.T
    sent_ref[...] = square_ref[0:EDGES, :]


def unpack_edges(got_ref, square_ref):
    row = lax.broadcasted_iota(jnp.int32, (EDGES, LANES), 0)
    square_ref[...] = jnp.zeros((LANES, LANES), jnp.float32)
    square_ref[0:EDGES, :] = jnp.where(lax.rem(row, SUB) < 2, got_ref[1], got_ref[0])
    square_ref[...] = square_ref[...].T


def settle(ref, sends, recvs):
    pltpu.make_async_copy(ref, ref, recvs).wait()
    pltpu.make_async_copy(ref, ref, sends).wait()


def over_line(gx, sent, got, sends, recvs):
    def one(turn, carry):
        apart = GX // 2 + (turn + 1) // 2 * (1 - 2 * (turn % 2))
        peer = lax.rem(gx + apart, GX)
        pltpu.make_async_remote_copy(
            src_ref=sent.at[peer],
            dst_ref=got.at[gx],
            send_sem=sends,
            recv_sem=recvs,
            device_id={"gx": peer},
            device_id_type=MESH,
        ).start()
        return carry

    lax.fori_loop(0, GX - 1, one, 0)
    got[gx] = sent[gx]
    settle(got.at[0 : GX - 1], sends, recvs)


def whole_kernel(
    flow_in,
    residual_in,
    speeds_in,
    dissip_in,
    to_in,
    from_in,
    ends_ref,
    kept,
    rows,
    from_modes,
    flow,
    residual,
    speeds,
    dissip,
    to_modes,
    scale,
    square,
    pack,
    edge_sent,
    edge_got,
    out_sent,
    out_got,
    back_sent,
    back_got,
    local_sem,
    halo_send,
    halo_recv,
    sends,
    recvs,
    relay,
):
    gx = lax.axis_index("gx")
    gy = lax.axis_index("gy")
    z = lax.div(gx, ALONG_Y)
    y = lax.rem(gx, ALONG_Y)
    has_up, has_down = gx > 0, gx < GX - 1
    has_left, has_right = gy > 0, gy < GY - 1

    barrier = pltpu.get_barrier_semaphore()

    def along_z(shift):
        return {"gx": lax.rem(z + ALONG_Z + shift, ALONG_Z) * ALONG_Y + y}

    def tell_z(semaphore, distance):
        for shift in (distance, -distance):
            pl.semaphore_signal(
                semaphore, 1, device_id=along_z(shift), device_id_type=MESH
            )

    tell_z(barrier, 1)
    for turn in range(1, ALONG_Y):
        peer = z * ALONG_Y + lax.rem(y + turn, ALONG_Y)
        pl.semaphore_signal(barrier, 1, device_id={"gx": peer}, device_id_type=MESH)
        peer = lax.rem(z + ALONG_Z - 1, ALONG_Z) * ALONG_Y + lax.rem(y + turn, ALONG_Y)
        pl.semaphore_signal(barrier, 1, device_id={"gx": peer}, device_id_type=MESH)
    for there, axis, peer in (
        (has_up, "gx", gx - 1),
        (has_down, "gx", gx + 1),
        (has_left, "gy", gy - 1),
        (has_right, "gy", gy + 1),
    ):

        @pl.when(there)
        def _(axis=axis, peer=peer):
            pl.semaphore_signal(barrier, 1, device_id={axis: peer}, device_id_type=MESH)

    inner = flow.at[:, LEAD : LEAD + ROWS, :]
    loads = [
        pltpu.make_async_copy(a, b, local_sem.at[i])
        for i, (a, b) in enumerate(
            (
                (speeds_in, speeds),
                (dissip_in, dissip),
                (flow_in, inner),
                (residual_in, residual),
                (to_in, to_modes),
                (from_in, from_modes),
            )
        )
    ]
    for load in loads:
        load.start()

    @pl.when(jnp.logical_not(has_up))
    def _():
        flow[:, 0:LEAD, :] = jnp.zeros((FIELDS, LEAD, LANES), jnp.float32)

    @pl.when(jnp.logical_not(has_down))
    def _():
        flow[:, LEAD + ROWS :, :] = jnp.zeros((FIELDS, LEAD, LANES), jnp.float32)

    @pl.when(jnp.logical_not(has_left))
    def _():
        edge_got[0] = jnp.zeros((EDGES, LANES), jnp.float32)

    @pl.when(jnp.logical_not(has_right))
    def _():
        edge_got[1] = jnp.zeros((EDGES, LANES), jnp.float32)

    for load in loads:
        load.wait()
    pack_edges(flow, square, edge_sent)

    near = (
        has_up.astype(jnp.int32)
        + has_down.astype(jnp.int32)
        + has_left.astype(jnp.int32)
        + has_right.astype(jnp.int32)
    )
    pl.semaphore_wait(barrier, 2 + 2 * (ALONG_Y - 1) + near)

    def halo(i, src, dst, target):
        return pltpu.make_async_remote_copy(
            src_ref=src,
            dst_ref=dst,
            send_sem=halo_send.at[i],
            recv_sem=halo_recv.at[i],
            device_id=target,
            device_id_type=MESH,
        )

    below = halo(0, flow_in.at[:, ROWS - LEAD :, :], flow.at[:, 0:LEAD, :], {"gx": gx + 1})
    above = halo(1, flow_in.at[:, 0:LEAD, :], flow.at[:, LEAD + ROWS :, :], {"gx": gx - 1})
    right = halo(2, edge_sent, edge_got.at[0], {"gy": gy + 1})
    left = halo(3, edge_sent, edge_got.at[1], {"gy": gy - 1})
    pairs = (
        (below, has_down, has_up),
        (above, has_up, has_down),
        (right, has_right, has_left),
        (left, has_left, has_right),
    )
    for copy, sending, _ in pairs:
        pl.when(sending)(copy.start)

    tell_z(relay.at[0], 1)
    state = factor(range(STEPS // 2), None, speeds, dissip, kept, scale)
    pl.semaphore_wait(relay.at[0], 2)
    tell_z(relay.at[1], 2)
    factor(range(STEPS // 2, STEPS), state, speeds, dissip, kept, scale)
    pl.semaphore_wait(relay.at[1], 2)
    tell_z(relay.at[2], 4)

    for copy, sending, receiving in pairs:
        pl.when(receiving)(copy.wait_recv)
        pl.when(sending)(copy.wait_send)

    unpack_edges(edge_got, square)
    sweep(flow, square, residual, dissip, to_modes, kept, scale)
    condense(kept, rows, pack)
    square[...] = pack[...].T
    for h in range(2):
        out_sent[:, h, :] = square[h * GX : (h + 1) * GX, :]
    pl.semaphore_wait(relay.at[2], 2)
    over_line(gx, out_sent, out_got, sends.at[0], recvs.at[0])
    for h in range(2):
        square[h * GX : (h + 1) * GX, :] = out_got[:, h, :]
    pack[...] = square[...].T
    solve_ends(pack, square)
    pack[...] = square[...].T
    back_sent[:, 0, :] = pack[0:GX, :] + pltpu.roll(pack[GX:, :], GX, 1)
    over_line(gx, back_sent, back_got, sends.at[1], recvs.at[1])
    square[0:GX, :] = back_got[:, 0, :]
    square[GX:, :] = pltpu.roll(square[0:GX, :], GX, 1)
    ends_ref[...] = square[...].T


def last_kernel(ends, kept, rows, from_modes, out):
    restore(ends, kept, rows, from_modes, out)


def local(flow_state, residual, speeds, dissip, to_modes, from_modes):
    f32 = jnp.float32
    block = (FIELDS, ROWS, LANES)
    vmem = pl.BlockSpec(memory_space=pltpu.VMEM)
    ends, kept, rows, modes_back = pl.pallas_call(
        whole_kernel,
        out_shape=(
            jax.ShapeDtypeStruct((LANES, LANES), f32),
            jax.ShapeDtypeStruct((FIELDS, STEPS, 5, SUB, LANES), f32),
            jax.ShapeDtypeStruct((FIELDS, 10, SUB, LANES), f32),
            jax.ShapeDtypeStruct((FIELDS, FIELDS, LANES), f32),
        ),
        in_specs=[pl.BlockSpec(memory_space=pltpu.HBM)] * 6,
        out_specs=(vmem,) * 4,
        scratch_shapes=[
            pltpu.VMEM((FIELDS, ROWS + 2 * LEAD, LANES), f32),
            pltpu.VMEM(block, f32),
            pltpu.VMEM(block, f32),
            pltpu.VMEM((ROWS, LANES), f32),
            pltpu.VMEM((FIELDS, FIELDS, LANES), f32),
            pltpu.VMEM((FIELDS, STEPS, 2, SUB, LANES), f32),
            pltpu.VMEM((LANES, LANES), f32),
            pltpu.VMEM((LANES, LANES), f32),
            pltpu.VMEM((EDGES, LANES), f32),
            pltpu.VMEM((2, EDGES, LANES), f32),
            pltpu.VMEM((GX, 2, LANES), f32),
            pltpu.VMEM((GX, 2, LANES), f32),
            pltpu.VMEM((GX, 1, LANES), f32),
            pltpu.VMEM((GX, 1, LANES), f32),
            pltpu.SemaphoreType.DMA((6,)),
            pltpu.SemaphoreType.DMA((4,)),
            pltpu.SemaphoreType.DMA((4,)),
            pltpu.SemaphoreType.DMA((2,)),
            pltpu.SemaphoreType.DMA((2,)),
            pltpu.SemaphoreType.REGULAR((3,)),
        ],
        compiler_params=pltpu.CompilerParams(
            collective_id=0, has_side_effects=True, vmem_limit_bytes=24 << 20
        ),
    )(
        *(
            pltpu.with_memory_space_constraint(a, pltpu.HBM)
            for a in (flow_state[0], residual[0], speeds[0], dissip[0], to_modes, from_modes)
        )
    )
    return pl.pallas_call(
        last_kernel,
        out_shape=jax.ShapeDtypeStruct(block, f32),
        in_specs=[vmem] * 4,
        out_specs=vmem,
        compiler_params=pltpu.CompilerParams(vmem_limit_bytes=24 << 20),
    )(ends, kept, rows, modes_back)[None]


def solution(mesh):
    placed = (
        P(None, None, "gx", "gy"),
        P(None, None, "gx", "gy"),
        P(None, None, "gx", "gy"),
        P(None, "gx", "gy"),
        P(None, None, "gy"),
        P(None, None, "gy"),
    )
    return jax.shard_map(
        local, mesh=mesh, in_specs=placed, out_specs=P(None, None, "gx", "gy"), check_vma=False
    )
```

```python
import jax
import jax.numpy as jnp
from jax import lax
from jax.experimental import pallas as pl
from jax.experimental.pallas import tpu as pltpu
from jax.sharding import PartitionSpec as P

explicit_gain = 4.0
wide_share = 0.5
FIELDS = 5
ROWS = 128
LANES = 128
SUB = 8
STEPS = ROWS // SUB
LEAD = 8
SLOT = 24
BACK = 4
ALONG_Y = 4
ALONG_Z = 16
GX = ALONG_Y * ALONG_Z
GY = 8
MESH = pl.DeviceIdType.MESH
EDGES = FIELDS * SUB


def mm(a, b):
    return tuple(
        tuple(a[i][0] * b[0][j] + a[i][1] * b[1][j] for j in range(2)) for i in range(2)
    )


def mv(a, v):
    return tuple(a[i][0] * v[0] + a[i][1] * v[1] for i in range(2))


def msub(a, b):
    return tuple(tuple(a[i][j] - b[i][j] for j in range(2)) for i in range(2))


def mneg(a):
    return tuple(tuple(-a[i][j] for j in range(2)) for i in range(2))


def vsub(a, b):
    return tuple(a[i] - b[i] for i in range(2))


def inverse_of_unit_less(a):
    upper = 1.0 - a[0][0]
    lower = 1.0 - a[1][1]
    scale = 1.0 / (upper * lower - a[0][1] * a[1][0])
    return ((lower * scale, a[0][1] * scale), (a[1][0] * scale, upper * scale))


def madd(a, b):
    return tuple(tuple(a[i][j] + b[i][j] for j in range(2)) for i in range(2))


def tree(fn, *items):
    return jax.tree.map(fn, *items)


def assemble(bottom, top_next):
    beta, c_mat, d_mat = bottom
    p_next, a_next, b_next = top_next
    solver = inverse_of_unit_less(mm(d_mat, a_next))
    return (
        mv(solver, vsub(beta, mv(d_mat, p_next))),
        mm(solver, c_mat),
        mneg(mm(solver, mm(d_mat, b_next))),
    )


def reduce_row(row, left, right):
    r, l_mat, r_mat = row
    solver = inverse_of_unit_less(madd(mm(l_mat, left[2]), mm(r_mat, right[1])))
    return (
        mv(solver, vsub(vsub(r, mv(l_mat, left[0])), mv(r_mat, right[0]))),
        mneg(mm(solver, mm(l_mat, left[1]))),
        mneg(mm(solver, mm(r_mat, right[2]))),
    )


def spread(row):
    return jnp.broadcast_to(row, (SUB, LANES))


def strided(ref, f, start):
    return ref[f, pl.ds(start, SUB, stride=STEPS), :]


def forcing_of(flow_ref, edge, residual_ref, damp, f, j, lane):
    mid = strided(flow_ref, f, LEAD + j)
    stream = (
        strided(flow_ref, f, LEAD + j - 2)
        - 4.0 * strided(flow_ref, f, LEAD + j - 1)
        + 6.0 * mid
        - 4.0 * strided(flow_ref, f, LEAD + j + 1)
        + strided(flow_ref, f, LEAD + j + 2)
    )
    back_two = jnp.where(lane < 2, edge, pltpu.roll(mid, 2, 1))
    back_one = jnp.where(lane < 1, pltpu.roll(edge, LANES - 1, 1), pltpu.roll(mid, 1, 1))
    next_one = jnp.where(lane >= LANES - 1, pltpu.roll(edge, 1, 1), pltpu.roll(mid, LANES - 1, 1))
    next_two = jnp.where(lane >= LANES - 2, edge, pltpu.roll(mid, LANES - 2, 1))
    cross = back_two - 4.0 * back_one + 6.0 * mid - 4.0 * next_one + next_two
    return strided(residual_ref, f, j) - explicit_gain * damp * (stream + cross)


def factor(steps, state, speeds_ref, dissip_ref, kept_ref, scale_ref):
    zero = jnp.zeros((SUB, LANES), jnp.float32)
    minus = zero - 1.0
    if state is None:
        state = (
            [(zero, zero, minus, zero) for _ in range(FIELDS)],
            [(zero, zero, zero, minus) for _ in range(FIELDS)],
        )
    old, last = state
    for j in steps:
        damp = dissip_ref[pl.ds(j, SUB, stride=STEPS), :]
        for f in range(FIELDS):
            speed = strided(speeds_ref, f, j)
            magnitude = jnp.abs(speed)
            near = damp * magnitude
            far = wide_share * near
            near_low = -(jnp.maximum(speed, 0.0) + near)
            centre = 1.0 + magnitude + 2.0 * near + 2.0 * far
            near_up = -(jnp.maximum(-speed, 0.0) + near)
            outer = -far
            reduced = near_low - outer * old[f][0]
            leading = centre - outer * old[f][1]
            pivot_inv = 1.0 / (leading - reduced * last[f][0])
            upper_two = outer * pivot_inv
            low = reduced * pivot_inv
            now = (
                (near_up - reduced * last[f][1]) * pivot_inv,
                upper_two,
                -(upper_two * old[f][2] + low * last[f][2]),
                -(upper_two * old[f][3] + low * last[f][3]),
            )
            for q in range(4):
                kept_ref[f, j, q] = now[q]
            scale_ref[f, j, 0] = pivot_inv
            scale_ref[f, j, 1] = low
            old[f], last[f] = last[f], now
    return old, last


def sweep(flow_ref, edge_ref, residual_ref, dissip_ref, to_ref, kept_ref, scale_ref):
    lane = lax.broadcasted_iota(jnp.int32, (SUB, LANES), 1)
    zero = jnp.zeros((SUB, LANES), jnp.float32)
    old = [zero] * FIELDS
    last = [zero] * FIELDS
    for j in range(STEPS):
        damp = dissip_ref[pl.ds(j, SUB, stride=STEPS), :]
        edges = edge_ref[pl.ds(j, SUB, stride=STEPS), :]
        forcing = [
            forcing_of(
                flow_ref,
                pltpu.roll(edges, LANES - 2 - SUB * f, 1),
                residual_ref,
                damp,
                f,
                j,
                lane,
            )
            for f in range(FIELDS)
        ]
        for f in range(FIELDS):
            modal = spread(to_ref[f, 0:1, :]) * forcing[0]
            for k in range(1, FIELDS):
                modal = modal + spread(to_ref[f, k : k + 1, :]) * forcing[k]
            now = (
                modal * scale_ref[f, j, 0]
                - kept_ref[f, j, 1] * old[f]
                - scale_ref[f, j, 1] * last[f]
            )
            kept_ref[f, j, 4] = now
            old[f], last[f] = last[f], now


def condense(kept_ref, rows_ref, pack_ref):
    sub = lax.broadcasted_iota(jnp.int32, (SUB, LANES), 0)
    zero = jnp.zeros((SUB, LANES), jnp.float32)
    minus = zero - 1.0
    none_vec = (zero, zero)
    none_mat = ((zero, zero), (zero, zero))
    minus_eye = ((minus, zero), (zero, minus))
    at_left = (none_vec, minus_eye, none_mat)
    at_right = (none_vec, none_mat, minus_eye)
    pack_ref[...] = jnp.zeros((LANES, LANES), jnp.float32)
    for f in range(FIELDS):
        u1a, u2a, z1a, z2a, ya = (kept_ref[f, STEPS - 2, q] for q in range(5))
        u1b, u2b, z1b, z2b, yb = (kept_ref[f, STEPS - 1, q] for q in range(5))
        beta = (ya - u1a * yb, yb)
        c_mat = ((z1a - u1a * z1b, z2a - u1a * z2b), (z1b, z2b))
        d_mat = ((u2a - u1a * u1b, -u1a * u2b), (u1b, u2b))
        nearer = (zero, zero, zero, minus, zero)
        farther = (zero, zero, zero, zero, minus)
        for j in reversed(range(STEPS - 2)):
            one = kept_ref[f, j, 0]
            two = kept_ref[f, j, 1]
            own = (kept_ref[f, j, 4], kept_ref[f, j, 2], kept_ref[f, j, 3])
            current = tuple(
                own[q] - one * nearer[q] - two * farther[q] for q in range(3)
            ) + tuple(-(one * nearer[q] + two * farther[q]) for q in range(3, 5))
            nearer, farther = current, nearer
        p_vec = (nearer[0], farther[0])
        a_mat = ((nearer[1], nearer[2]), (farther[1], farther[2]))
        b_mat = ((nearer[3], nearer[4]), (farther[3], farther[4]))
        top_next = tree(lambda a: pltpu.roll(a, SUB - 1, 0), (p_vec, a_mat, b_mat))
        row = assemble((beta, c_mat, d_mat), top_next)
        row = tree(lambda a, e: jnp.where(sub == SUB - 1, e, a), row, at_right)
        for step in (1, 2, 4):
            left = tree(lambda a, e: jnp.where(sub < step, e, pltpu.roll(a, step, 0)), row, at_left)
            right = tree(
                lambda a, e: jnp.where(sub >= SUB - 1 - step, e, pltpu.roll(a, SUB - step, 0)),
                row,
                at_right,
            )
            row = reduce_row(row, left, right)
        for q, a in enumerate(jax.tree.leaves(row)):
            rows_ref[f, q] = a
        top = (
            vsub(p_vec, mv(b_mat, row[0])),
            msub(a_mat, mm(b_mat, row[1])),
            mneg(mm(b_mat, row[2])),
        )
        before = tree(lambda a: pltpu.roll(a, 1, 0), row)
        solver = inverse_of_unit_less(mm(c_mat, before[2]))
        bottom = (
            mv(solver, vsub(beta, mv(c_mat, before[0]))),
            mneg(mm(solver, mm(c_mat, before[1]))),
            mm(solver, d_mat),
        )
        for q, a in enumerate(jax.tree.leaves(top)):
            pack_ref[f * SLOT + q : f * SLOT + q + 1, :] = a[0:1]
        for q, a in enumerate(jax.tree.leaves(bottom)):
            pack_ref[f * SLOT + 10 + q : f * SLOT + 11 + q, :] = a[SUB - 1 : SUB]


def as_relation(leaves):
    return (
        (leaves[0], leaves[1]),
        ((leaves[2], leaves[3]), (leaves[4], leaves[5])),
        ((leaves[6], leaves[7]), (leaves[8], leaves[9])),
    )


def solve_ends(pack_ref, back_ref):
    leaves = [pack_ref[pl.ds(q, FIELDS, stride=SLOT), :] for q in range(20)]
    place = lax.rem(lax.broadcasted_iota(jnp.int32, (FIELDS, LANES), 1), GX)

    def earlier(item, step):
        return tree(lambda a: jnp.where(place < step, 0.0, pltpu.roll(a, step, 1)), item)

    def later(item, step):
        return tree(
            lambda a: jnp.where(place >= GX - step, 0.0, pltpu.roll(a, LANES - step, 1)), item
        )

    row = assemble(as_relation(leaves[10:]), later(as_relation(leaves[:10]), 1))
    for step in (1, 2, 4, 8, 16, 32):
        row = reduce_row(row, earlier(row, step), later(row, step))
    own = row[0]
    back_ref[...] = jnp.zeros((LANES, LANES), jnp.float32)
    for v, a in enumerate(earlier(own, 1) + own):
        for f in range(FIELDS):
            back_ref[f * BACK + v : f * BACK + v + 1, :] = a[f : f + 1]


def restore(ends_ref, kept_ref, rows_ref, from_ref, out_ref):
    sub = lax.broadcasted_iota(jnp.int32, (SUB, LANES), 0)
    behind, state = [], []
    for f in range(FIELDS):
        edge = [spread(ends_ref[f * BACK + v : f * BACK + v + 1, :]) for v in range(BACK)]
        row = as_relation([rows_ref[f, q] for q in range(10)])
        cut = vsub(vsub(row[0], mv(row[1], edge[:2])), mv(row[2], edge[2:]))
        behind.append(
            tuple(jnp.where(sub == 0, edge[v], pltpu.roll(cut[v], 1, 0)) for v in range(2))
        )
        state.append(cut)
    for j in reversed(range(STEPS)):
        update = []
        for f in range(FIELDS):
            if j >= STEPS - 2:
                update.append(state[f][j - (STEPS - 2)])
                continue
            nearer, farther = state[f]
            current = (
                kept_ref[f, j, 4]
                - kept_ref[f, j, 2] * behind[f][0]
                - kept_ref[f, j, 3] * behind[f][1]
                - kept_ref[f, j, 1] * farther
                - kept_ref[f, j, 0] * nearer
            )
            state[f] = (current, nearer)
            update.append(current)
        for k in range(FIELDS):
            total = spread(from_ref[k, 0:1, :]) * update[0]
            for m in range(1, FIELDS):
                total = total + spread(from_ref[k, m : m + 1, :]) * update[m]
            out_ref[k, pl.ds(j, SUB, stride=STEPS), :] = total


def pack_edges(flow_ref, square_ref, sent_ref):
    lane = lax.broadcasted_iota(jnp.int32, (ROWS, LANES), 1)
    total = jnp.zeros((ROWS, LANES), jnp.float32)
    for f in range(FIELDS):
        mid = flow_ref[f, LEAD : LEAD + ROWS, :]
        at = lane - SUB * f
        total = jnp.where((at >= 0) & (at < 2), pltpu.roll(mid, SUB * f, 1) if f else mid, total)
        total = jnp.where((at >= 2) & (at < 4), pltpu.roll(mid, SUB * f + 4, 1), total)
    square_ref[...] = total.T
    sent_ref[...] = square_ref[0:EDGES, :]


def unpack_edges(got_ref, square_ref):
    row = lax.broadcasted_iota(jnp.int32, (EDGES, LANES), 0)
    square_ref[...] = jnp.zeros((LANES, LANES), jnp.float32)
    square_ref[0:EDGES, :] = jnp.where(lax.rem(row, SUB) < 2, got_ref[1], got_ref[0])
    square_ref[...] = square_ref[...].T


def settle(ref, sends, recvs):
    pltpu.make_async_copy(ref, ref, recvs).wait()
    pltpu.make_async_copy(ref, ref, sends).wait()


def over_line(gx, sent, got, sends, recvs):
    def one(turn, carry):
        apart = GX // 2 + (turn + 1) // 2 * (1 - 2 * (turn % 2))
        peer = lax.rem(gx + apart, GX)
        pltpu.make_async_remote_copy(
            src_ref=sent.at[peer],
            dst_ref=got.at[gx],
            send_sem=sends,
            recv_sem=recvs,
            device_id={"gx": peer},
            device_id_type=MESH,
        ).start()
        return carry

    lax.fori_loop(0, GX - 1, one, 0)
    got[gx] = sent[gx]
    settle(got.at[0 : GX - 1], sends, recvs)


def whole_kernel(
    flow_in,
    residual_in,
    speeds_in,
    dissip_in,
    to_in,
    from_in,
    ends_ref,
    kept,
    rows,
    from_modes,
    flow,
    residual,
    speeds,
    dissip,
    to_modes,
    scale,
    square,
    pack,
    edge_sent,
    edge_got,
    out_sent,
    out_got,
    back_sent,
    back_got,
    local_sem,
    halo_send,
    halo_recv,
    sends,
    recvs,
    relay,
    ready,
):
    gx = lax.axis_index("gx")
    gy = lax.axis_index("gy")
    z = lax.div(gx, ALONG_Y)
    y = lax.rem(gx, ALONG_Y)
    has_up, has_down = gx > 0, gx < GX - 1
    has_left, has_right = gy > 0, gy < GY - 1

    barrier = pltpu.get_barrier_semaphore()

    def along_z(shift):
        return {"gx": lax.rem(z + ALONG_Z + shift, ALONG_Z) * ALONG_Y + y}

    def tell_z(semaphore, distance):
        for shift in (distance, -distance):
            pl.semaphore_signal(
                semaphore, 1, device_id=along_z(shift), device_id_type=MESH
            )

    tell_z(barrier, 1)
    for turn in range(1, ALONG_Y):
        peer = z * ALONG_Y + lax.rem(y + turn, ALONG_Y)
        pl.semaphore_signal(barrier, 1, device_id={"gx": peer}, device_id_type=MESH)
        peer = lax.rem(z + ALONG_Z - 1, ALONG_Z) * ALONG_Y + lax.rem(y + turn, ALONG_Y)
        pl.semaphore_signal(barrier, 1, device_id={"gx": peer}, device_id_type=MESH)
    for there, peer in ((has_up, gx - 1), (has_down, gx + 1)):

        @pl.when(there)
        def _(peer=peer):
            pl.semaphore_signal(barrier, 1, device_id={"gx": peer}, device_id_type=MESH)

    def tell_sides(semaphore, condition):
        for there, peer in ((has_left, gy - 1), (has_right, gy + 1)):

            @pl.when(condition & there)
            def _(peer=peer):
                pl.semaphore_signal(semaphore, 1, device_id={"gy": peer}, device_id_type=MESH)

    inner = flow.at[:, LEAD : LEAD + ROWS, :]
    loads = [
        pltpu.make_async_copy(a, b, local_sem.at[i])
        for i, (a, b) in enumerate(
            (
                (speeds_in, speeds),
                (dissip_in, dissip),
                (flow_in, inner),
                (residual_in, residual),
                (to_in, to_modes),
                (from_in, from_modes),
            )
        )
    ]
    for load in loads:
        load.start()

    @pl.when(jnp.logical_not(has_up))
    def _():
        flow[:, 0:LEAD, :] = jnp.zeros((FIELDS, LEAD, LANES), jnp.float32)

    @pl.when(jnp.logical_not(has_down))
    def _():
        flow[:, LEAD + ROWS :, :] = jnp.zeros((FIELDS, LEAD, LANES), jnp.float32)

    @pl.when(jnp.logical_not(has_left))
    def _():
        edge_got[0] = jnp.zeros((EDGES, LANES), jnp.float32)

    @pl.when(jnp.logical_not(has_right))
    def _():
        edge_got[1] = jnp.zeros((EDGES, LANES), jnp.float32)

    for load in loads:
        load.wait()
    pack_edges(flow, square, edge_sent)

    near = has_up.astype(jnp.int32) + has_down.astype(jnp.int32)
    beside = has_left.astype(jnp.int32) + has_right.astype(jnp.int32)
    odd = lax.rem(gy, 2)
    even_line = odd == 0
    odd_line = odd == 1
    pl.semaphore_wait(barrier, 2 + 2 * (ALONG_Y - 1) + near + odd * beside)
    tell_sides(barrier, even_line)
    tell_sides(ready.at[0], odd_line)

    def halo(i, src, dst, target):
        return pltpu.make_async_remote_copy(
            src_ref=src,
            dst_ref=dst,
            send_sem=halo_send.at[i],
            recv_sem=halo_recv.at[i],
            device_id=target,
            device_id_type=MESH,
        )

    below = halo(0, flow_in.at[:, ROWS - LEAD :, :], flow.at[:, 0:LEAD, :], {"gx": gx + 1})
    above = halo(1, flow_in.at[:, 0:LEAD, :], flow.at[:, LEAD + ROWS :, :], {"gx": gx - 1})
    right = halo(2, edge_sent, edge_got.at[0], {"gy": gy + 1})
    left = halo(3, edge_sent, edge_got.at[1], {"gy": gy - 1})
    pairs = (
        (below, has_down, has_up),
        (above, has_up, has_down),
        (right, has_right, has_left),
        (left, has_left, has_right),
    )
    for copy, sending, _ in pairs[:2]:
        pl.when(sending)(copy.start)
    for copy, sending, _ in pairs[2:]:
        pl.when(odd_line & sending)(copy.start)

    tell_z(relay.at[0], 1)
    state = factor(range(STEPS // 2), None, speeds, dissip, kept, scale)
    pl.semaphore_wait(relay.at[0], 2)
    tell_z(relay.at[1], 2)
    factor(range(STEPS // 2, STEPS), state, speeds, dissip, kept, scale)
    pl.semaphore_wait(relay.at[1], 2)
    tell_z(relay.at[2], 4)

    @pl.when(even_line)
    def _():
        pl.semaphore_wait(ready.at[0], beside)

    for copy, sending, _ in pairs[2:]:
        pl.when(even_line & sending)(copy.start)
    for copy, sending, receiving in pairs:
        pl.when(receiving)(copy.wait_recv)
        pl.when(sending)(copy.wait_send)

    unpack_edges(edge_got, square)
    sweep(flow, square, residual, dissip, to_modes, kept, scale)
    condense(kept, rows, pack)
    square[...] = pack[...].T
    for h in range(2):
        out_sent[:, h, :] = square[h * GX : (h + 1) * GX, :]
    pl.semaphore_wait(relay.at[2], 2)
    over_line(gx, out_sent, out_got, sends.at[0], recvs.at[0])
    for h in range(2):
        square[h * GX : (h + 1) * GX, :] = out_got[:, h, :]
    pack[...] = square[...].T
    solve_ends(pack, square)
    pack[...] = square[...].T
    back_sent[:, 0, :] = pack[0:GX, :] + pltpu.roll(pack[GX:, :], GX, 1)
    over_line(gx, back_sent, back_got, sends.at[1], recvs.at[1])
    square[0:GX, :] = back_got[:, 0, :]
    square[GX:, :] = pltpu.roll(square[0:GX, :], GX, 1)
    ends_ref[...] = square[...].T


def last_kernel(ends, kept, rows, from_modes, out):
    restore(ends, kept, rows, from_modes, out)


def local(flow_state, residual, speeds, dissip, to_modes, from_modes):
    f32 = jnp.float32
    block = (FIELDS, ROWS, LANES)
    vmem = pl.BlockSpec(memory_space=pltpu.VMEM)
    ends, kept, rows, modes_back = pl.pallas_call(
        whole_kernel,
        out_shape=(
            jax.ShapeDtypeStruct((LANES, LANES), f32),
            jax.ShapeDtypeStruct((FIELDS, STEPS, 5, SUB, LANES), f32),
            jax.ShapeDtypeStruct((FIELDS, 10, SUB, LANES), f32),
            jax.ShapeDtypeStruct((FIELDS, FIELDS, LANES), f32),
        ),
        in_specs=[pl.BlockSpec(memory_space=pltpu.HBM)] * 6,
        out_specs=(vmem,) * 4,
        scratch_shapes=[
            pltpu.VMEM((FIELDS, ROWS + 2 * LEAD, LANES), f32),
            pltpu.VMEM(block, f32),
            pltpu.VMEM(block, f32),
            pltpu.VMEM((ROWS, LANES), f32),
            pltpu.VMEM((FIELDS, FIELDS, LANES), f32),
            pltpu.VMEM((FIELDS, STEPS, 2, SUB, LANES), f32),
            pltpu.VMEM((LANES, LANES), f32),
            pltpu.VMEM((LANES, LANES), f32),
            pltpu.VMEM((EDGES, LANES), f32),
            pltpu.VMEM((2, EDGES, LANES), f32),
            pltpu.VMEM((GX, 2, LANES), f32),
            pltpu.VMEM((GX, 2, LANES), f32),
            pltpu.VMEM((GX, 1, LANES), f32),
            pltpu.VMEM((GX, 1, LANES), f32),
            pltpu.SemaphoreType.DMA((6,)),
            pltpu.SemaphoreType.DMA((4,)),
            pltpu.SemaphoreType.DMA((4,)),
            pltpu.SemaphoreType.DMA((2,)),
            pltpu.SemaphoreType.DMA((2,)),
            pltpu.SemaphoreType.REGULAR((3,)),
            pltpu.SemaphoreType.REGULAR((1,)),
        ],
        compiler_params=pltpu.CompilerParams(
            collective_id=0, has_side_effects=True, vmem_limit_bytes=24 << 20
        ),
    )(
        *(
            pltpu.with_memory_space_constraint(a, pltpu.HBM)
            for a in (flow_state[0], residual[0], speeds[0], dissip[0], to_modes, from_modes)
        )
    )
    return pl.pallas_call(
        last_kernel,
        out_shape=jax.ShapeDtypeStruct(block, f32),
        in_specs=[vmem] * 4,
        out_specs=vmem,
        compiler_params=pltpu.CompilerParams(vmem_limit_bytes=24 << 20),
    )(ends, kept, rows, modes_back)[None]


def solution(mesh):
    placed = (
        P(None, None, "gx", "gy"),
        P(None, None, "gx", "gy"),
        P(None, None, "gx", "gy"),
        P(None, "gx", "gy"),
        P(None, None, "gy"),
        P(None, None, "gy"),
    )
    return jax.shard_map(
        local, mesh=mesh, in_specs=placed, out_specs=P(None, None, "gx", "gy"), check_vma=False
    )
```

```python
import jax
import jax.numpy as jnp
from jax import lax
from jax.experimental import pallas as pl
from jax.experimental.pallas import tpu as pltpu
from jax.sharding import PartitionSpec as P

explicit_gain = 4.0
wide_share = 0.5
FIELDS = 5
ROWS = 128
LANES = 128
SUB = 8
STEPS = ROWS // SUB
LEAD = 8
SLOT = 24
BACK = 4
ALONG_Y = 4
ALONG_Z = 16
GX = ALONG_Y * ALONG_Z
GY = 8
MESH = pl.DeviceIdType.MESH
EDGES = FIELDS * SUB


def mm(a, b):
    return tuple(
        tuple(a[i][0] * b[0][j] + a[i][1] * b[1][j] for j in range(2)) for i in range(2)
    )


def mv(a, v):
    return tuple(a[i][0] * v[0] + a[i][1] * v[1] for i in range(2))


def msub(a, b):
    return tuple(tuple(a[i][j] - b[i][j] for j in range(2)) for i in range(2))


def mneg(a):
    return tuple(tuple(-a[i][j] for j in range(2)) for i in range(2))


def vsub(a, b):
    return tuple(a[i] - b[i] for i in range(2))


def inverse_of_unit_less(a):
    upper = 1.0 - a[0][0]
    lower = 1.0 - a[1][1]
    scale = 1.0 / (upper * lower - a[0][1] * a[1][0])
    return ((lower * scale, a[0][1] * scale), (a[1][0] * scale, upper * scale))


def madd(a, b):
    return tuple(tuple(a[i][j] + b[i][j] for j in range(2)) for i in range(2))


def tree(fn, *items):
    return jax.tree.map(fn, *items)


def assemble(bottom, top_next):
    beta, c_mat, d_mat = bottom
    p_next, a_next, b_next = top_next
    solver = inverse_of_unit_less(mm(d_mat, a_next))
    return (
        mv(solver, vsub(beta, mv(d_mat, p_next))),
        mm(solver, c_mat),
        mneg(mm(solver, mm(d_mat, b_next))),
    )


def reduce_row(row, left, right):
    r, l_mat, r_mat = row
    solver = inverse_of_unit_less(madd(mm(l_mat, left[2]), mm(r_mat, right[1])))
    return (
        mv(solver, vsub(vsub(r, mv(l_mat, left[0])), mv(r_mat, right[0]))),
        mneg(mm(solver, mm(l_mat, left[1]))),
        mneg(mm(solver, mm(r_mat, right[2]))),
    )


def spread(row):
    return jnp.broadcast_to(row, (SUB, LANES))


def strided(ref, f, start):
    return ref[f, pl.ds(start, SUB, stride=STEPS), :]


def forcing_of(flow_ref, edge, residual_ref, damp, f, j, lane):
    mid = strided(flow_ref, f, LEAD + j)
    stream = (
        strided(flow_ref, f, LEAD + j - 2)
        - 4.0 * strided(flow_ref, f, LEAD + j - 1)
        + 6.0 * mid
        - 4.0 * strided(flow_ref, f, LEAD + j + 1)
        + strided(flow_ref, f, LEAD + j + 2)
    )
    back_two = jnp.where(lane < 2, edge, pltpu.roll(mid, 2, 1))
    back_one = jnp.where(lane < 1, pltpu.roll(edge, LANES - 1, 1), pltpu.roll(mid, 1, 1))
    next_one = jnp.where(lane >= LANES - 1, pltpu.roll(edge, 1, 1), pltpu.roll(mid, LANES - 1, 1))
    next_two = jnp.where(lane >= LANES - 2, edge, pltpu.roll(mid, LANES - 2, 1))
    cross = back_two - 4.0 * back_one + 6.0 * mid - 4.0 * next_one + next_two
    return strided(residual_ref, f, j) - explicit_gain * damp * (stream + cross)


def factor(steps, state, speeds_ref, dissip_ref, kept_ref, scale_ref):
    zero = jnp.zeros((SUB, LANES), jnp.float32)
    minus = zero - 1.0
    if state is None:
        state = (
            [(zero, zero, minus, zero) for _ in range(FIELDS)],
            [(zero, zero, zero, minus) for _ in range(FIELDS)],
        )
    old, last = state
    for j in steps:
        damp = dissip_ref[pl.ds(j, SUB, stride=STEPS), :]
        for f in range(FIELDS):
            speed = strided(speeds_ref, f, j)
            magnitude = jnp.abs(speed)
            near = damp * magnitude
            far = wide_share * near
            near_low = -(jnp.maximum(speed, 0.0) + near)
            centre = 1.0 + magnitude + 2.0 * near + 2.0 * far
            near_up = -(jnp.maximum(-speed, 0.0) + near)
            outer = -far
            reduced = near_low - outer * old[f][0]
            leading = centre - outer * old[f][1]
            pivot_inv = 1.0 / (leading - reduced * last[f][0])
            upper_two = outer * pivot_inv
            low = reduced * pivot_inv
            now = (
                (near_up - reduced * last[f][1]) * pivot_inv,
                upper_two,
                -(upper_two * old[f][2] + low * last[f][2]),
                -(upper_two * old[f][3] + low * last[f][3]),
            )
            for q in range(4):
                kept_ref[f, j, q] = now[q]
            scale_ref[f, j, 0] = pivot_inv
            scale_ref[f, j, 1] = low
            old[f], last[f] = last[f], now
    return old, last


def sweep(flow_ref, edge_ref, residual_ref, dissip_ref, to_ref, kept_ref, scale_ref):
    lane = lax.broadcasted_iota(jnp.int32, (SUB, LANES), 1)
    zero = jnp.zeros((SUB, LANES), jnp.float32)
    old = [zero] * FIELDS
    last = [zero] * FIELDS
    for j in range(STEPS):
        damp = dissip_ref[pl.ds(j, SUB, stride=STEPS), :]
        edges = edge_ref[pl.ds(j, SUB, stride=STEPS), :]
        forcing = [
            forcing_of(
                flow_ref,
                pltpu.roll(edges, LANES - 2 - SUB * f, 1),
                residual_ref,
                damp,
                f,
                j,
                lane,
            )
            for f in range(FIELDS)
        ]
        for f in range(FIELDS):
            modal = spread(to_ref[f, 0:1, :]) * forcing[0]
            for k in range(1, FIELDS):
                modal = modal + spread(to_ref[f, k : k + 1, :]) * forcing[k]
            now = (
                modal * scale_ref[f, j, 0]
                - kept_ref[f, j, 1] * old[f]
                - scale_ref[f, j, 1] * last[f]
            )
            kept_ref[f, j, 4] = now
            old[f], last[f] = last[f], now


def store_mats(ref, f, first, *mats):
    for q, a in enumerate(jax.tree.leaves(mats)):
        ref[f, first + q] = a


def load_mat(ref, f, first):
    return ((ref[f, first], ref[f, first + 1]), (ref[f, first + 2], ref[f, first + 3]))


def pack_row(pack_ref, f, q, a, at):
    pack_ref[f * SLOT + q : f * SLOT + q + 1, :] = a[at : at + 1]


def condense_matrices(kept_ref, mats_ref, rows_ref, pack_ref):
    sub = lax.broadcasted_iota(jnp.int32, (SUB, LANES), 0)
    zero = jnp.zeros((SUB, LANES), jnp.float32)
    minus = zero - 1.0
    none_mat = ((zero, zero), (zero, zero))
    minus_eye = ((minus, zero), (zero, minus))
    at_left = (minus_eye, none_mat)
    at_right = (none_mat, minus_eye)
    pack_ref[...] = jnp.zeros((LANES, LANES), jnp.float32)
    for f in range(FIELDS):
        u1a, u2a, z1a, z2a = (kept_ref[f, STEPS - 2, q] for q in range(4))
        u1b, u2b, z1b, z2b = (kept_ref[f, STEPS - 1, q] for q in range(4))
        c_mat = ((z1a - u1a * z1b, z2a - u1a * z2b), (z1b, z2b))
        d_mat = ((u2a - u1a * u1b, -u1a * u2b), (u1b, u2b))
        nearer = (zero, zero, minus, zero)
        farther = (zero, zero, zero, minus)
        for j in reversed(range(STEPS - 2)):
            one = kept_ref[f, j, 0]
            two = kept_ref[f, j, 1]
            current = tuple(
                kept_ref[f, j, 2 + q] - one * nearer[q] - two * farther[q] for q in range(2)
            ) + tuple(-(one * nearer[q] + two * farther[q]) for q in range(2, 4))
            nearer, farther = current, nearer
        a_mat = ((nearer[0], nearer[1]), (farther[0], farther[1]))
        b_mat = ((nearer[2], nearer[3]), (farther[2], farther[3]))
        a_next, b_next = tree(lambda a: pltpu.roll(a, SUB - 1, 0), (a_mat, b_mat))
        solver = inverse_of_unit_less(mm(d_mat, a_next))
        store_mats(mats_ref, f, 0, c_mat, d_mat, b_mat, solver)
        row = (mm(solver, c_mat), mneg(mm(solver, mm(d_mat, b_next))))
        row = tree(lambda a, e: jnp.where(sub == SUB - 1, e, a), row, at_right)
        for i, step in enumerate((1, 2, 4)):
            left = tree(lambda a, e: jnp.where(sub < step, e, pltpu.roll(a, step, 0)), row, at_left)
            right = tree(
                lambda a, e: jnp.where(sub >= SUB - 1 - step, e, pltpu.roll(a, SUB - step, 0)),
                row,
                at_right,
            )
            solver = inverse_of_unit_less(madd(mm(row[0], left[1]), mm(row[1], right[0])))
            store_mats(mats_ref, f, 20 + 12 * i, solver, row)
            row = (
                mneg(mm(solver, mm(row[0], left[0]))),
                mneg(mm(solver, mm(row[1], right[1]))),
            )
        store_mats(rows_ref, f, 2, row)
        before = tree(lambda a: pltpu.roll(a, 1, 0), row)
        solver = inverse_of_unit_less(mm(c_mat, before[1]))
        store_mats(mats_ref, f, 16, solver)
        top = (msub(a_mat, mm(b_mat, row[0])), mneg(mm(b_mat, row[1])))
        bottom = (mneg(mm(solver, mm(c_mat, before[0]))), mm(solver, d_mat))
        for q, a in enumerate(jax.tree.leaves(top)):
            pack_row(pack_ref, f, 2 + q, a, 0)
        for q, a in enumerate(jax.tree.leaves(bottom)):
            pack_row(pack_ref, f, 12 + q, a, SUB - 1)


def condense_vectors(kept_ref, mats_ref, rows_ref, pack_ref):
    sub = lax.broadcasted_iota(jnp.int32, (SUB, LANES), 0)
    zero = jnp.zeros((SUB, LANES), jnp.float32)
    for f in range(FIELDS):
        c_mat, d_mat, b_mat, solver, last_solver = (
            load_mat(mats_ref, f, 4 * q) for q in range(5)
        )
        value = kept_ref[f, STEPS - 1, 4]
        beta = (kept_ref[f, STEPS - 2, 4] - kept_ref[f, STEPS - 2, 0] * value, value)
        nearer, farther = zero, zero
        for j in reversed(range(STEPS - 2)):
            nearer, farther = (
                kept_ref[f, j, 4] - kept_ref[f, j, 0] * nearer - kept_ref[f, j, 1] * farther,
                nearer,
            )
        p_vec = (nearer, farther)
        p_next = tree(lambda a: pltpu.roll(a, SUB - 1, 0), p_vec)
        r = mv(solver, vsub(beta, mv(d_mat, p_next)))
        r = tree(lambda a: jnp.where(sub == SUB - 1, 0.0, a), r)
        for i, step in enumerate((1, 2, 4)):
            solver, l_mat, r_mat = (load_mat(mats_ref, f, 20 + 12 * i + 4 * q) for q in range(3))
            left = tree(lambda a: jnp.where(sub < step, 0.0, pltpu.roll(a, step, 0)), r)
            right = tree(
                lambda a: jnp.where(sub >= SUB - 1 - step, 0.0, pltpu.roll(a, SUB - step, 0)), r
            )
            r = mv(solver, vsub(vsub(r, mv(l_mat, left)), mv(r_mat, right)))
        before = tree(lambda a: pltpu.roll(a, 1, 0), r)
        top = vsub(p_vec, mv(b_mat, r))
        bottom = mv(last_solver, vsub(beta, mv(c_mat, before)))
        for q in range(2):
            rows_ref[f, q] = r[q]
            pack_row(pack_ref, f, q, top[q], 0)
            pack_row(pack_ref, f, 10 + q, bottom[q], SUB - 1)


def as_relation(leaves):
    return (
        (leaves[0], leaves[1]),
        ((leaves[2], leaves[3]), (leaves[4], leaves[5])),
        ((leaves[6], leaves[7]), (leaves[8], leaves[9])),
    )


def solve_ends(pack_ref, back_ref):
    leaves = [pack_ref[pl.ds(q, FIELDS, stride=SLOT), :] for q in range(20)]
    place = lax.rem(lax.broadcasted_iota(jnp.int32, (FIELDS, LANES), 1), GX)

    def earlier(item, step):
        return tree(lambda a: jnp.where(place < step, 0.0, pltpu.roll(a, step, 1)), item)

    def later(item, step):
        return tree(
            lambda a: jnp.where(place >= GX - step, 0.0, pltpu.roll(a, LANES - step, 1)), item
        )

    row = assemble(as_relation(leaves[10:]), later(as_relation(leaves[:10]), 1))
    for step in (1, 2, 4, 8, 16, 32):
        row = reduce_row(row, earlier(row, step), later(row, step))
    own = row[0]
    back_ref[...] = jnp.zeros((LANES, LANES), jnp.float32)
    for v, a in enumerate(earlier(own, 1) + own):
        for f in range(FIELDS):
            back_ref[f * BACK + v : f * BACK + v + 1, :] = a[f : f + 1]


def restore(ends_ref, kept_ref, rows_ref, from_ref, out_ref):
    sub = lax.broadcasted_iota(jnp.int32, (SUB, LANES), 0)
    behind, state = [], []
    for f in range(FIELDS):
        edge = [spread(ends_ref[f * BACK + v : f * BACK + v + 1, :]) for v in range(BACK)]
        row = as_relation([rows_ref[f, q] for q in range(10)])
        cut = vsub(vsub(row[0], mv(row[1], edge[:2])), mv(row[2], edge[2:]))
        behind.append(
            tuple(jnp.where(sub == 0, edge[v], pltpu.roll(cut[v], 1, 0)) for v in range(2))
        )
        state.append(cut)
    for j in reversed(range(STEPS)):
        update = []
        for f in range(FIELDS):
            if j >= STEPS - 2:
                update.append(state[f][j - (STEPS - 2)])
                continue
            nearer, farther = state[f]
            current = (
                kept_ref[f, j, 4]
                - kept_ref[f, j, 2] * behind[f][0]
                - kept_ref[f, j, 3] * behind[f][1]
                - kept_ref[f, j, 1] * farther
                - kept_ref[f, j, 0] * nearer
            )
            state[f] = (current, nearer)
            update.append(current)
        for k in range(FIELDS):
            total = spread(from_ref[k, 0:1, :]) * update[0]
            for m in range(1, FIELDS):
                total = total + spread(from_ref[k, m : m + 1, :]) * update[m]
            out_ref[k, pl.ds(j, SUB, stride=STEPS), :] = total


def pack_edges(flow_ref, square_ref, sent_ref):
    lane = lax.broadcasted_iota(jnp.int32, (ROWS, LANES), 1)
    total = jnp.zeros((ROWS, LANES), jnp.float32)
    for f in range(FIELDS):
        mid = flow_ref[f, LEAD : LEAD + ROWS, :]
        at = lane - SUB * f
        total = jnp.where((at >= 0) & (at < 2), pltpu.roll(mid, SUB * f, 1) if f else mid, total)
        total = jnp.where((at >= 2) & (at < 4), pltpu.roll(mid, SUB * f + 4, 1), total)
    square_ref[...] = total.T
    sent_ref[...] = square_ref[0:EDGES, :]


def unpack_edges(got_ref, square_ref):
    row = lax.broadcasted_iota(jnp.int32, (EDGES, LANES), 0)
    square_ref[...] = jnp.zeros((LANES, LANES), jnp.float32)
    square_ref[0:EDGES, :] = jnp.where(lax.rem(row, SUB) < 2, got_ref[1], got_ref[0])
    square_ref[...] = square_ref[...].T


def settle(ref, sends, recvs):
    pltpu.make_async_copy(ref, ref, recvs).wait()
    pltpu.make_async_copy(ref, ref, sends).wait()


def over_line(gx, sent, got, sends, recvs):
    def one(turn, carry):
        apart = GX // 2 + (turn + 1) // 2 * (1 - 2 * (turn % 2))
        peer = lax.rem(gx + apart, GX)
        pltpu.make_async_remote_copy(
            src_ref=sent.at[peer],
            dst_ref=got.at[gx],
            send_sem=sends,
            recv_sem=recvs,
            device_id={"gx": peer},
            device_id_type=MESH,
        ).start()
        return carry

    lax.fori_loop(0, GX - 1, one, 0)
    got[gx] = sent[gx]
    settle(got.at[0 : GX - 1], sends, recvs)


def whole_kernel(
    flow_in,
    residual_in,
    speeds_in,
    dissip_in,
    to_in,
    from_in,
    ends_ref,
    kept,
    rows,
    from_modes,
    flow,
    residual,
    speeds,
    dissip,
    to_modes,
    scale,
    mats,
    square,
    pack,
    edge_sent,
    edge_got,
    out_sent,
    out_got,
    back_sent,
    back_got,
    local_sem,
    halo_send,
    halo_recv,
    sends,
    recvs,
    relay,
):
    gx = lax.axis_index("gx")
    gy = lax.axis_index("gy")
    z = lax.div(gx, ALONG_Y)
    y = lax.rem(gx, ALONG_Y)
    has_up, has_down = gx > 0, gx < GX - 1
    has_left, has_right = gy > 0, gy < GY - 1

    barrier = pltpu.get_barrier_semaphore()

    def along_z(shift):
        return {"gx": lax.rem(z + ALONG_Z + shift, ALONG_Z) * ALONG_Y + y}

    def tell_z(semaphore, distance):
        for shift in (distance, -distance):
            pl.semaphore_signal(
                semaphore, 1, device_id=along_z(shift), device_id_type=MESH
            )

    tell_z(barrier, 1)
    for turn in range(1, ALONG_Y):
        peer = z * ALONG_Y + lax.rem(y + turn, ALONG_Y)
        pl.semaphore_signal(barrier, 1, device_id={"gx": peer}, device_id_type=MESH)
        peer = lax.rem(z + ALONG_Z - 1, ALONG_Z) * ALONG_Y + lax.rem(y + turn, ALONG_Y)
        pl.semaphore_signal(barrier, 1, device_id={"gx": peer}, device_id_type=MESH)
    for there, axis, peer in (
        (has_up, "gx", gx - 1),
        (has_down, "gx", gx + 1),
        (has_left, "gy", gy - 1),
        (has_right, "gy", gy + 1),
    ):

        @pl.when(there)
        def _(axis=axis, peer=peer):
            pl.semaphore_signal(barrier, 1, device_id={axis: peer}, device_id_type=MESH)

    inner = flow.at[:, LEAD : LEAD + ROWS, :]
    loads = [
        pltpu.make_async_copy(a, b, local_sem.at[i])
        for i, (a, b) in enumerate(
            (
                (speeds_in, speeds),
                (dissip_in, dissip),
                (flow_in, inner),
                (residual_in, residual),
                (to_in, to_modes),
                (from_in, from_modes),
            )
        )
    ]
    for load in loads:
        load.start()

    @pl.when(jnp.logical_not(has_up))
    def _():
        flow[:, 0:LEAD, :] = jnp.zeros((FIELDS, LEAD, LANES), jnp.float32)

    @pl.when(jnp.logical_not(has_down))
    def _():
        flow[:, LEAD + ROWS :, :] = jnp.zeros((FIELDS, LEAD, LANES), jnp.float32)

    @pl.when(jnp.logical_not(has_left))
    def _():
        edge_got[0] = jnp.zeros((EDGES, LANES), jnp.float32)

    @pl.when(jnp.logical_not(has_right))
    def _():
        edge_got[1] = jnp.zeros((EDGES, LANES), jnp.float32)

    for load in loads:
        load.wait()
    pack_edges(flow, square, edge_sent)

    near = (
        has_up.astype(jnp.int32)
        + has_down.astype(jnp.int32)
        + has_left.astype(jnp.int32)
        + has_right.astype(jnp.int32)
    )
    pl.semaphore_wait(barrier, 2 + 2 * (ALONG_Y - 1) + near)

    def halo(i, src, dst, target):
        return pltpu.make_async_remote_copy(
            src_ref=src,
            dst_ref=dst,
            send_sem=halo_send.at[i],
            recv_sem=halo_recv.at[i],
            device_id=target,
            device_id_type=MESH,
        )

    below = halo(0, flow_in.at[:, ROWS - LEAD :, :], flow.at[:, 0:LEAD, :], {"gx": gx + 1})
    above = halo(1, flow_in.at[:, 0:LEAD, :], flow.at[:, LEAD + ROWS :, :], {"gx": gx - 1})
    right = halo(2, edge_sent, edge_got.at[0], {"gy": gy + 1})
    left = halo(3, edge_sent, edge_got.at[1], {"gy": gy - 1})
    pairs = (
        (below, has_down, has_up),
        (above, has_up, has_down),
        (right, has_right, has_left),
        (left, has_left, has_right),
    )
    tell_z(relay.at[0], 1)
    for copy, sending, _ in pairs:
        pl.when(sending)(copy.start)
    state = factor(range(STEPS // 2), None, speeds, dissip, kept, scale)
    pl.semaphore_wait(relay.at[0], 2)
    tell_z(relay.at[1], 2)
    factor(range(STEPS // 2, STEPS), state, speeds, dissip, kept, scale)
    pl.semaphore_wait(relay.at[1], 2)
    tell_z(relay.at[2], 4)
    condense_matrices(kept, mats, rows, pack)
    for copy, _, receiving in pairs:
        pl.when(receiving)(copy.wait_recv)

    unpack_edges(edge_got, square)
    sweep(flow, square, residual, dissip, to_modes, kept, scale)
    condense_vectors(kept, mats, rows, pack)
    square[...] = pack[...].T
    for h in range(2):
        out_sent[:, h, :] = square[h * GX : (h + 1) * GX, :]
    pl.semaphore_wait(relay.at[2], 2)
    over_line(gx, out_sent, out_got, sends.at[0], recvs.at[0])
    for h in range(2):
        square[h * GX : (h + 1) * GX, :] = out_got[:, h, :]
    pack[...] = square[...].T
    solve_ends(pack, square)
    pack[...] = square[...].T
    back_sent[:, 0, :] = pack[0:GX, :] + pltpu.roll(pack[GX:, :], GX, 1)
    over_line(gx, back_sent, back_got, sends.at[1], recvs.at[1])
    square[0:GX, :] = back_got[:, 0, :]
    square[GX:, :] = pltpu.roll(square[0:GX, :], GX, 1)
    ends_ref[...] = square[...].T
    for copy, sending, _ in pairs:
        pl.when(sending)(copy.wait_send)


def last_kernel(ends, kept, rows, from_modes, out):
    restore(ends, kept, rows, from_modes, out)


def local(flow_state, residual, speeds, dissip, to_modes, from_modes):
    f32 = jnp.float32
    block = (FIELDS, ROWS, LANES)
    vmem = pl.BlockSpec(memory_space=pltpu.VMEM)
    ends, kept, rows, modes_back = pl.pallas_call(
        whole_kernel,
        out_shape=(
            jax.ShapeDtypeStruct((LANES, LANES), f32),
            jax.ShapeDtypeStruct((FIELDS, STEPS, 5, SUB, LANES), f32),
            jax.ShapeDtypeStruct((FIELDS, 10, SUB, LANES), f32),
            jax.ShapeDtypeStruct((FIELDS, FIELDS, LANES), f32),
        ),
        in_specs=[pl.BlockSpec(memory_space=pltpu.HBM)] * 6,
        out_specs=(vmem,) * 4,
        scratch_shapes=[
            pltpu.VMEM((FIELDS, ROWS + 2 * LEAD, LANES), f32),
            pltpu.VMEM(block, f32),
            pltpu.VMEM(block, f32),
            pltpu.VMEM((ROWS, LANES), f32),
            pltpu.VMEM((FIELDS, FIELDS, LANES), f32),
            pltpu.VMEM((FIELDS, STEPS, 2, SUB, LANES), f32),
            pltpu.VMEM((FIELDS, 56, SUB, LANES), f32),
            pltpu.VMEM((LANES, LANES), f32),
            pltpu.VMEM((LANES, LANES), f32),
            pltpu.VMEM((EDGES, LANES), f32),
            pltpu.VMEM((2, EDGES, LANES), f32),
            pltpu.VMEM((GX, 2, LANES), f32),
            pltpu.VMEM((GX, 2, LANES), f32),
            pltpu.VMEM((GX, 1, LANES), f32),
            pltpu.VMEM((GX, 1, LANES), f32),
            pltpu.SemaphoreType.DMA((6,)),
            pltpu.SemaphoreType.DMA((4,)),
            pltpu.SemaphoreType.DMA((4,)),
            pltpu.SemaphoreType.DMA((2,)),
            pltpu.SemaphoreType.DMA((2,)),
            pltpu.SemaphoreType.REGULAR((3,)),
        ],
        compiler_params=pltpu.CompilerParams(
            collective_id=0, has_side_effects=True, vmem_limit_bytes=24 << 20
        ),
    )(
        *(
            pltpu.with_memory_space_constraint(a, pltpu.HBM)
            for a in (flow_state[0], residual[0], speeds[0], dissip[0], to_modes, from_modes)
        )
    )
    return pl.pallas_call(
        last_kernel,
        out_shape=jax.ShapeDtypeStruct(block, f32),
        in_specs=[vmem] * 4,
        out_specs=vmem,
        compiler_params=pltpu.CompilerParams(vmem_limit_bytes=24 << 20),
    )(ends, kept, rows, modes_back)[None]


def solution(mesh):
    placed = (
        P(None, None, "gx", "gy"),
        P(None, None, "gx", "gy"),
        P(None, None, "gx", "gy"),
        P(None, "gx", "gy"),
        P(None, None, "gy"),
        P(None, None, "gy"),
    )
    return jax.shard_map(
        local, mesh=mesh, in_specs=placed, out_specs=P(None, None, "gx", "gy"), check_vma=False
    )
```

```python
import jax
import jax.numpy as jnp
from jax import lax
from jax.experimental import pallas as pl
from jax.experimental.pallas import tpu as pltpu
from jax.sharding import PartitionSpec as P

explicit_gain = 4.0
wide_share = 0.5
FIELDS = 5
ROWS = 128
LANES = 128
SUB = 8
STEPS = ROWS // SUB
LEAD = 8
SLOT = 24
BACK = 4
ALONG_Y = 4
ALONG_Z = 16
GX = ALONG_Y * ALONG_Z
GY = 8
MESH = pl.DeviceIdType.MESH
EDGES = FIELDS * SUB


def mm(a, b):
    return tuple(
        tuple(a[i][0] * b[0][j] + a[i][1] * b[1][j] for j in range(2)) for i in range(2)
    )


def mv(a, v):
    return tuple(a[i][0] * v[0] + a[i][1] * v[1] for i in range(2))


def msub(a, b):
    return tuple(tuple(a[i][j] - b[i][j] for j in range(2)) for i in range(2))


def mneg(a):
    return tuple(tuple(-a[i][j] for j in range(2)) for i in range(2))


def vsub(a, b):
    return tuple(a[i] - b[i] for i in range(2))


def inverse_of_unit_less(a):
    upper = 1.0 - a[0][0]
    lower = 1.0 - a[1][1]
    scale = 1.0 / (upper * lower - a[0][1] * a[1][0])
    return ((lower * scale, a[0][1] * scale), (a[1][0] * scale, upper * scale))


def madd(a, b):
    return tuple(tuple(a[i][j] + b[i][j] for j in range(2)) for i in range(2))


def tree(fn, *items):
    return jax.tree.map(fn, *items)


def assemble(bottom, top_next):
    beta, c_mat, d_mat = bottom
    p_next, a_next, b_next = top_next
    solver = inverse_of_unit_less(mm(d_mat, a_next))
    return (
        mv(solver, vsub(beta, mv(d_mat, p_next))),
        mm(solver, c_mat),
        mneg(mm(solver, mm(d_mat, b_next))),
    )


def reduce_row(row, left, right):
    r, l_mat, r_mat = row
    solver = inverse_of_unit_less(madd(mm(l_mat, left[2]), mm(r_mat, right[1])))
    return (
        mv(solver, vsub(vsub(r, mv(l_mat, left[0])), mv(r_mat, right[0]))),
        mneg(mm(solver, mm(l_mat, left[1]))),
        mneg(mm(solver, mm(r_mat, right[2]))),
    )


def spread(row):
    return jnp.broadcast_to(row, (SUB, LANES))


def strided(ref, f, start):
    return ref[f, pl.ds(start, SUB, stride=STEPS), :]


def forcing_of(flow_ref, edge, residual_ref, damp, f, j, lane):
    mid = strided(flow_ref, f, LEAD + j)
    stream = (
        strided(flow_ref, f, LEAD + j - 2)
        - 4.0 * strided(flow_ref, f, LEAD + j - 1)
        + 6.0 * mid
        - 4.0 * strided(flow_ref, f, LEAD + j + 1)
        + strided(flow_ref, f, LEAD + j + 2)
    )
    back_two = jnp.where(lane < 2, edge, pltpu.roll(mid, 2, 1))
    back_one = jnp.where(lane < 1, pltpu.roll(edge, LANES - 1, 1), pltpu.roll(mid, 1, 1))
    next_one = jnp.where(lane >= LANES - 1, pltpu.roll(edge, 1, 1), pltpu.roll(mid, LANES - 1, 1))
    next_two = jnp.where(lane >= LANES - 2, edge, pltpu.roll(mid, LANES - 2, 1))
    cross = back_two - 4.0 * back_one + 6.0 * mid - 4.0 * next_one + next_two
    return strided(residual_ref, f, j) - explicit_gain * damp * (stream + cross)


def factor(steps, state, speeds_ref, dissip_ref, kept_ref, scale_ref):
    zero = jnp.zeros((SUB, LANES), jnp.float32)
    minus = zero - 1.0
    if state is None:
        state = (
            [(zero, zero, minus, zero) for _ in range(FIELDS)],
            [(zero, zero, zero, minus) for _ in range(FIELDS)],
        )
    old, last = state
    for j in steps:
        damp = dissip_ref[pl.ds(j, SUB, stride=STEPS), :]
        for f in range(FIELDS):
            speed = strided(speeds_ref, f, j)
            magnitude = jnp.abs(speed)
            near = damp * magnitude
            far = wide_share * near
            near_low = -(jnp.maximum(speed, 0.0) + near)
            centre = 1.0 + magnitude + 2.0 * near + 2.0 * far
            near_up = -(jnp.maximum(-speed, 0.0) + near)
            outer = -far
            reduced = near_low - outer * old[f][0]
            leading = centre - outer * old[f][1]
            pivot_inv = 1.0 / (leading - reduced * last[f][0])
            upper_two = outer * pivot_inv
            low = reduced * pivot_inv
            now = (
                (near_up - reduced * last[f][1]) * pivot_inv,
                upper_two,
                -(upper_two * old[f][2] + low * last[f][2]),
                -(upper_two * old[f][3] + low * last[f][3]),
            )
            for q in range(4):
                kept_ref[f, j, q] = now[q]
            scale_ref[f, j, 0] = pivot_inv
            scale_ref[f, j, 1] = low
            old[f], last[f] = last[f], now
    return old, last


def sweep(flow_ref, edge_ref, residual_ref, dissip_ref, to_ref, kept_ref, scale_ref):
    lane = lax.broadcasted_iota(jnp.int32, (SUB, LANES), 1)
    zero = jnp.zeros((SUB, LANES), jnp.float32)
    old = [zero] * FIELDS
    last = [zero] * FIELDS
    for j in range(STEPS):
        damp = dissip_ref[pl.ds(j, SUB, stride=STEPS), :]
        edges = edge_ref[pl.ds(j, SUB, stride=STEPS), :]
        forcing = [
            forcing_of(
                flow_ref,
                pltpu.roll(edges, LANES - 2 - SUB * f, 1),
                residual_ref,
                damp,
                f,
                j,
                lane,
            )
            for f in range(FIELDS)
        ]
        for f in range(FIELDS):
            modal = spread(to_ref[f, 0:1, :]) * forcing[0]
            for k in range(1, FIELDS):
                modal = modal + spread(to_ref[f, k : k + 1, :]) * forcing[k]
            now = (
                modal * scale_ref[f, j, 0]
                - kept_ref[f, j, 1] * old[f]
                - scale_ref[f, j, 1] * last[f]
            )
            kept_ref[f, j, 4] = now
            old[f], last[f] = last[f], now


def store_mats(ref, f, first, *mats):
    for q, a in enumerate(jax.tree.leaves(mats)):
        ref[f, first + q] = a


def load_mat(ref, f, first):
    return ((ref[f, first], ref[f, first + 1]), (ref[f, first + 2], ref[f, first + 3]))


def pack_row(pack_ref, f, q, a, at):
    pack_ref[f * SLOT + q : f * SLOT + q + 1, :] = a[at : at + 1]


def condense_matrices(kept_ref, mats_ref, rows_ref, pack_ref):
    sub = lax.broadcasted_iota(jnp.int32, (SUB, LANES), 0)
    zero = jnp.zeros((SUB, LANES), jnp.float32)
    minus = zero - 1.0
    none_mat = ((zero, zero), (zero, zero))
    minus_eye = ((minus, zero), (zero, minus))
    at_left = (minus_eye, none_mat)
    at_right = (none_mat, minus_eye)
    pack_ref[...] = jnp.zeros((LANES, LANES), jnp.float32)
    for f in range(FIELDS):
        u1a, u2a, z1a, z2a = (kept_ref[f, STEPS - 2, q] for q in range(4))
        u1b, u2b, z1b, z2b = (kept_ref[f, STEPS - 1, q] for q in range(4))
        c_mat = ((z1a - u1a * z1b, z2a - u1a * z2b), (z1b, z2b))
        d_mat = ((u2a - u1a * u1b, -u1a * u2b), (u1b, u2b))
        nearer = (zero, zero, minus, zero)
        farther = (zero, zero, zero, minus)
        for j in reversed(range(STEPS - 2)):
            one = kept_ref[f, j, 0]
            two = kept_ref[f, j, 1]
            current = tuple(
                kept_ref[f, j, 2 + q] - one * nearer[q] - two * farther[q] for q in range(2)
            ) + tuple(-(one * nearer[q] + two * farther[q]) for q in range(2, 4))
            nearer, farther = current, nearer
        a_mat = ((nearer[0], nearer[1]), (farther[0], farther[1]))
        b_mat = ((nearer[2], nearer[3]), (farther[2], farther[3]))
        a_next, b_next = tree(lambda a: pltpu.roll(a, SUB - 1, 0), (a_mat, b_mat))
        solver = inverse_of_unit_less(mm(d_mat, a_next))
        store_mats(mats_ref, f, 0, c_mat, d_mat, b_mat, solver)
        row = (mm(solver, c_mat), mneg(mm(solver, mm(d_mat, b_next))))
        row = tree(lambda a, e: jnp.where(sub == SUB - 1, e, a), row, at_right)
        for i, step in enumerate((1, 2, 4)):
            left = tree(lambda a, e: jnp.where(sub < step, e, pltpu.roll(a, step, 0)), row, at_left)
            right = tree(
                lambda a, e: jnp.where(sub >= SUB - 1 - step, e, pltpu.roll(a, SUB - step, 0)),
                row,
                at_right,
            )
            solver = inverse_of_unit_less(madd(mm(row[0], left[1]), mm(row[1], right[0])))
            store_mats(mats_ref, f, 20 + 12 * i, solver, row)
            row = (
                mneg(mm(solver, mm(row[0], left[0]))),
                mneg(mm(solver, mm(row[1], right[1]))),
            )
        store_mats(rows_ref, f, 2, row)
        before = tree(lambda a: pltpu.roll(a, 1, 0), row)
        solver = inverse_of_unit_less(mm(c_mat, before[1]))
        store_mats(mats_ref, f, 16, solver)
        top = (msub(a_mat, mm(b_mat, row[0])), mneg(mm(b_mat, row[1])))
        bottom = (mneg(mm(solver, mm(c_mat, before[0]))), mm(solver, d_mat))
        for q, a in enumerate(jax.tree.leaves(top)):
            pack_row(pack_ref, f, 2 + q, a, 0)
        for q, a in enumerate(jax.tree.leaves(bottom)):
            pack_row(pack_ref, f, 12 + q, a, SUB - 1)


def condense_vectors(kept_ref, mats_ref, rows_ref, pack_ref):
    sub = lax.broadcasted_iota(jnp.int32, (SUB, LANES), 0)
    zero = jnp.zeros((SUB, LANES), jnp.float32)
    for f in range(FIELDS):
        c_mat, d_mat, b_mat, solver, last_solver = (
            load_mat(mats_ref, f, 4 * q) for q in range(5)
        )
        value = kept_ref[f, STEPS - 1, 4]
        beta = (kept_ref[f, STEPS - 2, 4] - kept_ref[f, STEPS - 2, 0] * value, value)
        nearer, farther = zero, zero
        for j in reversed(range(STEPS - 2)):
            nearer, farther = (
                kept_ref[f, j, 4] - kept_ref[f, j, 0] * nearer - kept_ref[f, j, 1] * farther,
                nearer,
            )
        p_vec = (nearer, farther)
        p_next = tree(lambda a: pltpu.roll(a, SUB - 1, 0), p_vec)
        r = mv(solver, vsub(beta, mv(d_mat, p_next)))
        r = tree(lambda a: jnp.where(sub == SUB - 1, 0.0, a), r)
        for i, step in enumerate((1, 2, 4)):
            solver, l_mat, r_mat = (load_mat(mats_ref, f, 20 + 12 * i + 4 * q) for q in range(3))
            left = tree(lambda a: jnp.where(sub < step, 0.0, pltpu.roll(a, step, 0)), r)
            right = tree(
                lambda a: jnp.where(sub >= SUB - 1 - step, 0.0, pltpu.roll(a, SUB - step, 0)), r
            )
            r = mv(solver, vsub(vsub(r, mv(l_mat, left)), mv(r_mat, right)))
        before = tree(lambda a: pltpu.roll(a, 1, 0), r)
        top = vsub(p_vec, mv(b_mat, r))
        bottom = mv(last_solver, vsub(beta, mv(c_mat, before)))
        for q in range(2):
            rows_ref[f, q] = r[q]
            pack_row(pack_ref, f, q, top[q], 0)
            pack_row(pack_ref, f, 10 + q, bottom[q], SUB - 1)


def as_relation(leaves):
    return (
        (leaves[0], leaves[1]),
        ((leaves[2], leaves[3]), (leaves[4], leaves[5])),
        ((leaves[6], leaves[7]), (leaves[8], leaves[9])),
    )


def solve_ends(pack_ref, back_ref):
    leaves = [pack_ref[pl.ds(q, FIELDS, stride=SLOT), :] for q in range(20)]
    place = lax.rem(lax.broadcasted_iota(jnp.int32, (FIELDS, LANES), 1), GX)

    def earlier(item, step):
        return tree(lambda a: jnp.where(place < step, 0.0, pltpu.roll(a, step, 1)), item)

    def later(item, step):
        return tree(
            lambda a: jnp.where(place >= GX - step, 0.0, pltpu.roll(a, LANES - step, 1)), item
        )

    row = assemble(as_relation(leaves[10:]), later(as_relation(leaves[:10]), 1))
    for step in (1, 2, 4, 8, 16, 32):
        row = reduce_row(row, earlier(row, step), later(row, step))
    own = row[0]
    back_ref[...] = jnp.zeros((LANES, LANES), jnp.float32)
    for v, a in enumerate(earlier(own, 1) + own):
        for f in range(FIELDS):
            back_ref[f * BACK + v : f * BACK + v + 1, :] = a[f : f + 1]


def restore(ends_ref, kept_ref, rows_ref, from_ref, out_ref):
    sub = lax.broadcasted_iota(jnp.int32, (SUB, LANES), 0)
    behind, state = [], []
    for f in range(FIELDS):
        edge = [spread(ends_ref[f * BACK + v : f * BACK + v + 1, :]) for v in range(BACK)]
        row = as_relation([rows_ref[f, q] for q in range(10)])
        cut = vsub(vsub(row[0], mv(row[1], edge[:2])), mv(row[2], edge[2:]))
        behind.append(
            tuple(jnp.where(sub == 0, edge[v], pltpu.roll(cut[v], 1, 0)) for v in range(2))
        )
        state.append(cut)
    for j in reversed(range(STEPS)):
        update = []
        for f in range(FIELDS):
            if j >= STEPS - 2:
                update.append(state[f][j - (STEPS - 2)])
                continue
            nearer, farther = state[f]
            current = (
                kept_ref[f, j, 4]
                - kept_ref[f, j, 2] * behind[f][0]
                - kept_ref[f, j, 3] * behind[f][1]
                - kept_ref[f, j, 1] * farther
                - kept_ref[f, j, 0] * nearer
            )
            state[f] = (current, nearer)
            update.append(current)
        for k in range(FIELDS):
            total = spread(from_ref[k, 0:1, :]) * update[0]
            for m in range(1, FIELDS):
                total = total + spread(from_ref[k, m : m + 1, :]) * update[m]
            out_ref[k, pl.ds(j, SUB, stride=STEPS), :] = total


def pack_edges(flow_ref, square_ref, sent_ref):
    lane = lax.broadcasted_iota(jnp.int32, (ROWS, LANES), 1)
    total = jnp.zeros((ROWS, LANES), jnp.float32)
    for f in range(FIELDS):
        mid = flow_ref[f, LEAD : LEAD + ROWS, :]
        at = lane - SUB * f
        total = jnp.where((at >= 0) & (at < 2), pltpu.roll(mid, SUB * f, 1) if f else mid, total)
        total = jnp.where((at >= 2) & (at < 4), pltpu.roll(mid, SUB * f + 4, 1), total)
    square_ref[...] = total.T
    sent_ref[...] = square_ref[0:EDGES, :]


def unpack_edges(got_ref, square_ref):
    row = lax.broadcasted_iota(jnp.int32, (EDGES, LANES), 0)
    square_ref[...] = jnp.zeros((LANES, LANES), jnp.float32)
    square_ref[0:EDGES, :] = jnp.where(lax.rem(row, SUB) < 2, got_ref[1], got_ref[0])
    square_ref[...] = square_ref[...].T


def settle(ref, sends, recvs):
    pltpu.make_async_copy(ref, ref, recvs).wait()
    pltpu.make_async_copy(ref, ref, sends).wait()


def over_line(gx, sent, got, sends, recvs):
    def one(turn):
        apart = GX // 2 + (turn + 1) // 2 * (1 - 2 * (turn % 2))
        peer = lax.rem(gx + apart, GX)
        pltpu.make_async_remote_copy(
            src_ref=sent.at[peer],
            dst_ref=got.at[gx],
            send_sem=sends,
            recv_sem=recvs,
            device_id={"gx": peer},
            device_id_type=MESH,
        ).start()

    def trip(index, carry):
        for inner in range(7):
            one(7 * index + inner)
        return carry

    lax.fori_loop(0, (GX - 1) // 7, trip, 0)
    got[gx] = sent[gx]
    settle(got.at[0 : GX - 1], sends, recvs)


def whole_kernel(
    flow_in,
    residual_in,
    speeds_in,
    dissip_in,
    to_in,
    from_in,
    ends_ref,
    kept,
    rows,
    from_modes,
    flow,
    residual,
    speeds,
    dissip,
    to_modes,
    scale,
    mats,
    square,
    pack,
    edge_sent,
    edge_got,
    out_sent,
    out_got,
    back_sent,
    back_got,
    local_sem,
    halo_send,
    halo_recv,
    sends,
    recvs,
    relay,
):
    gx = lax.axis_index("gx")
    gy = lax.axis_index("gy")
    z = lax.div(gx, ALONG_Y)
    y = lax.rem(gx, ALONG_Y)
    has_up, has_down = gx > 0, gx < GX - 1
    has_left, has_right = gy > 0, gy < GY - 1

    barrier = pltpu.get_barrier_semaphore()

    def along_z(shift):
        return {"gx": lax.rem(z + ALONG_Z + shift, ALONG_Z) * ALONG_Y + y}

    def tell_z(semaphore, distance):
        for shift in (distance, -distance):
            pl.semaphore_signal(
                semaphore, 1, device_id=along_z(shift), device_id_type=MESH
            )

    tell_z(barrier, 1)
    for turn in range(1, ALONG_Y):
        peer = z * ALONG_Y + lax.rem(y + turn, ALONG_Y)
        pl.semaphore_signal(barrier, 1, device_id={"gx": peer}, device_id_type=MESH)
        peer = lax.rem(z + ALONG_Z - 1, ALONG_Z) * ALONG_Y + lax.rem(y + turn, ALONG_Y)
        pl.semaphore_signal(barrier, 1, device_id={"gx": peer}, device_id_type=MESH)
    for there, axis, peer in (
        (has_up, "gx", gx - 1),
        (has_down, "gx", gx + 1),
        (has_left, "gy", gy - 1),
        (has_right, "gy", gy + 1),
    ):

        @pl.when(there)
        def _(axis=axis, peer=peer):
            pl.semaphore_signal(barrier, 1, device_id={axis: peer}, device_id_type=MESH)

    inner = flow.at[:, LEAD : LEAD + ROWS, :]
    loads = [
        pltpu.make_async_copy(a, b, local_sem.at[i])
        for i, (a, b) in enumerate(
            (
                (speeds_in, speeds),
                (dissip_in, dissip),
                (flow_in, inner),
                (residual_in, residual),
                (to_in, to_modes),
                (from_in, from_modes),
            )
        )
    ]
    for load in loads:
        load.start()

    @pl.when(jnp.logical_not(has_up))
    def _():
        flow[:, 0:LEAD, :] = jnp.zeros((FIELDS, LEAD, LANES), jnp.float32)

    @pl.when(jnp.logical_not(has_down))
    def _():
        flow[:, LEAD + ROWS :, :] = jnp.zeros((FIELDS, LEAD, LANES), jnp.float32)

    @pl.when(jnp.logical_not(has_left))
    def _():
        edge_got[0] = jnp.zeros((EDGES, LANES), jnp.float32)

    @pl.when(jnp.logical_not(has_right))
    def _():
        edge_got[1] = jnp.zeros((EDGES, LANES), jnp.float32)

    for load in loads:
        load.wait()
    pack_edges(flow, square, edge_sent)

    near = (
        has_up.astype(jnp.int32)
        + has_down.astype(jnp.int32)
        + has_left.astype(jnp.int32)
        + has_right.astype(jnp.int32)
    )
    pl.semaphore_wait(barrier, 2 + 2 * (ALONG_Y - 1) + near)

    def halo(i, src, dst, target):
        return pltpu.make_async_remote_copy(
            src_ref=src,
            dst_ref=dst,
            send_sem=halo_send.at[i],
            recv_sem=halo_recv.at[i],
            device_id=target,
            device_id_type=MESH,
        )

    below = halo(0, flow_in.at[:, ROWS - LEAD :, :], flow.at[:, 0:LEAD, :], {"gx": gx + 1})
    above = halo(1, flow_in.at[:, 0:LEAD, :], flow.at[:, LEAD + ROWS :, :], {"gx": gx - 1})
    right = halo(2, edge_sent, edge_got.at[0], {"gy": gy + 1})
    left = halo(3, edge_sent, edge_got.at[1], {"gy": gy - 1})
    pairs = (
        (below, has_down, has_up),
        (above, has_up, has_down),
        (right, has_right, has_left),
        (left, has_left, has_right),
    )
    tell_z(relay.at[0], 1)
    for copy, sending, _ in pairs:
        pl.when(sending)(copy.start)
    state = factor(range(STEPS // 2), None, speeds, dissip, kept, scale)
    pl.semaphore_wait(relay.at[0], 2)
    tell_z(relay.at[1], 2)
    factor(range(STEPS // 2, STEPS), state, speeds, dissip, kept, scale)
    pl.semaphore_wait(relay.at[1], 2)
    tell_z(relay.at[2], 4)
    condense_matrices(kept, mats, rows, pack)
    for copy, _, receiving in pairs:
        pl.when(receiving)(copy.wait_recv)

    unpack_edges(edge_got, square)
    sweep(flow, square, residual, dissip, to_modes, kept, scale)
    condense_vectors(kept, mats, rows, pack)
    square[...] = pack[...].T
    for h in range(2):
        out_sent[:, h, :] = square[h * GX : (h + 1) * GX, :]
    pl.semaphore_wait(relay.at[2], 2)
    over_line(gx, out_sent, out_got, sends.at[0], recvs.at[0])
    for h in range(2):
        square[h * GX : (h + 1) * GX, :] = out_got[:, h, :]
    pack[...] = square[...].T
    solve_ends(pack, square)
    pack[...] = square[...].T
    back_sent[:, 0, :] = pack[0:GX, :] + pltpu.roll(pack[GX:, :], GX, 1)
    over_line(gx, back_sent, back_got, sends.at[1], recvs.at[1])
    square[0:GX, :] = back_got[:, 0, :]
    square[GX:, :] = pltpu.roll(square[0:GX, :], GX, 1)
    ends_ref[...] = square[...].T
    for copy, sending, _ in pairs:
        pl.when(sending)(copy.wait_send)


def last_kernel(ends, kept, rows, from_modes, out):
    restore(ends, kept, rows, from_modes, out)


def local(flow_state, residual, speeds, dissip, to_modes, from_modes):
    f32 = jnp.float32
    block = (FIELDS, ROWS, LANES)
    vmem = pl.BlockSpec(memory_space=pltpu.VMEM)
    ends, kept, rows, modes_back = pl.pallas_call(
        whole_kernel,
        out_shape=(
            jax.ShapeDtypeStruct((LANES, LANES), f32),
            jax.ShapeDtypeStruct((FIELDS, STEPS, 5, SUB, LANES), f32),
            jax.ShapeDtypeStruct((FIELDS, 10, SUB, LANES), f32),
            jax.ShapeDtypeStruct((FIELDS, FIELDS, LANES), f32),
        ),
        in_specs=[pl.BlockSpec(memory_space=pltpu.HBM)] * 6,
        out_specs=(vmem,) * 4,
        scratch_shapes=[
            pltpu.VMEM((FIELDS, ROWS + 2 * LEAD, LANES), f32),
            pltpu.VMEM(block, f32),
            pltpu.VMEM(block, f32),
            pltpu.VMEM((ROWS, LANES), f32),
            pltpu.VMEM((FIELDS, FIELDS, LANES), f32),
            pltpu.VMEM((FIELDS, STEPS, 2, SUB, LANES), f32),
            pltpu.VMEM((FIELDS, 56, SUB, LANES), f32),
            pltpu.VMEM((LANES, LANES), f32),
            pltpu.VMEM((LANES, LANES), f32),
            pltpu.VMEM((EDGES, LANES), f32),
            pltpu.VMEM((2, EDGES, LANES), f32),
            pltpu.VMEM((GX, 2, LANES), f32),
            pltpu.VMEM((GX, 2, LANES), f32),
            pltpu.VMEM((GX, 1, LANES), f32),
            pltpu.VMEM((GX, 1, LANES), f32),
            pltpu.SemaphoreType.DMA((6,)),
            pltpu.SemaphoreType.DMA((4,)),
            pltpu.SemaphoreType.DMA((4,)),
            pltpu.SemaphoreType.DMA((2,)),
            pltpu.SemaphoreType.DMA((2,)),
            pltpu.SemaphoreType.REGULAR((3,)),
        ],
        compiler_params=pltpu.CompilerParams(
            collective_id=0, has_side_effects=True, vmem_limit_bytes=24 << 20
        ),
    )(
        *(
            pltpu.with_memory_space_constraint(a, pltpu.HBM)
            for a in (flow_state[0], residual[0], speeds[0], dissip[0], to_modes, from_modes)
        )
    )
    return pl.pallas_call(
        last_kernel,
        out_shape=jax.ShapeDtypeStruct(block, f32),
        in_specs=[vmem] * 4,
        out_specs=vmem,
        compiler_params=pltpu.CompilerParams(vmem_limit_bytes=24 << 20),
    )(ends, kept, rows, modes_back)[None]


def solution(mesh):
    placed = (
        P(None, None, "gx", "gy"),
        P(None, None, "gx", "gy"),
        P(None, None, "gx", "gy"),
        P(None, "gx", "gy"),
        P(None, None, "gy"),
        P(None, None, "gy"),
    )
    return jax.shard_map(
        local, mesh=mesh, in_specs=placed, out_specs=P(None, None, "gx", "gy"), check_vma=False
    )
```
